256 devices in a mesh: dp: 16 (over z, core), expert: 16 (over y, x).
Axes of the slice: x: 4, y: 4, z: 8, core: 2. Of those that a mesh axis runs over, the one named last changes fastest.
Arguments:
- tokens: bfloat16 [32768, 1024], P(('dp', 'expert')), may hold values from -6 to 6
- routes: int32 [32768, 8], P(('dp', 'expert')), may hold values from 0 to 63, all different within a row; in each aligned block of 128 rows (0 to 127, 128 to 255, ...) at most 24 rows name the same one
- gates: float32 [32768, 8], P(('dp', 'expert')), may hold values from 0.02 to 0.3
- cotangent: bfloat16 [32768, 1024], P(('dp', 'expert')), may hold values from -6 to 6
- w_gate: bfloat16 [64, 1024, 384], P('expert', 'dp'), may hold values from -0.1875 to 0.1875
- w_up: bfloat16 [64, 1024, 384], P('expert', 'dp'), may hold values from -0.1875 to 0.1875
- w_down: bfloat16 [64, 384, 1024], P('expert', None, 'dp'), may hold values from -0.3125 to 0.3125
Outputs:
- mixed: bfloat16 [32768, 1024], P(('dp', 'expert'))
- input_grad: bfloat16 [32768, 1024], P(('dp', 'expert'))
- gate_grads: float32 [32768, 8], P(('dp', 'expert'))
- grad_gate: float32 [64, 1024, 384], P('expert', 'dp')
- grad_up: float32 [64, 1024, 384], P('expert', 'dp')
- grad_down: float32 [64, 384, 1024], P('expert', None, 'dp')
The draws below stay inside these ranges and needn't reach their ends.
Inputs may be any that keep to these rules, and one draw needn't show every extreme that they name: `routes`: each row names 8 different experts; within the rows of one device no expert is named more than 24 times, a bound that some block reaches.
All inputs are finite; a program needn't handle non-finite values.
Results may differ from the reference program's by a relative error of at most 0.02.
Values may be sent and summed in bfloat16 or wider, within the bound.
A program may use at most 128 MiB of HBM per device.

```python
import math
import jax
import jax.numpy as jnp
import numpy as np
from jax import lax

D = 1024
H = 384
TOP = 8
TOK_DEV = 128
EXPERTS = 64
CAP = 24
TOKENS = 32768
N_DP = 16
N_EXPERT = 16


def level_of(stream_key, extent, split, smallest, high):
    gain, own = 1.0, jax.random.fold_in(stream_key, 6)
    for dim, shards_of in split:
        draws = jnp.exp(jax.random.uniform(jax.random.fold_in(own, dim), (shards_of,), jnp.float32, smallest / len(split), high / len(split)))
        gain = gain * jnp.repeat(draws, extent[dim] // shards_of).reshape([-1 if axis == dim else 1 for axis in range(len(extent))])
    return gain


def assign_block(own_key, own, number, rows, count, top, most, slope):
    sequence = jax.random.permutation(own_key, count)
    packed, usual = portions_of(count, rows * top, most, slope, True), portions_of(count, rows * top, most, slope, False)
    places = jnp.arange(count)

    def named(tallies, rotation):
        used = int((tallies > 0).sum())
        fixed = max(1, used // 4)
        moved = fixed + (places - fixed + rotation * (used - fixed)) % max(1, count - fixed)
        return jnp.zeros((count,), jnp.int32).at[sequence[jnp.where(places < fixed, places, moved)]].set(jnp.asarray(tallies, jnp.int32))

    tallies = jnp.where(number % 4 == 0, named(packed, number // 4), named(usual, number - number // 4 - 1))
    mixed = jax.random.permutation(jax.random.fold_in(own, 3), count)
    giver, receiver = mixed[0:count // 2 * 2:2], mixed[1:count // 2 * 2:2]
    margin = jnp.minimum(tallies[giver] - 1, most - tallies[receiver]) // 2
    margin = jnp.where((giver == sequence[0]) | (receiver == sequence[0]) | (tallies[receiver] == 0), 0, jnp.maximum(margin, 0))
    moved = jax.random.randint(jax.random.fold_in(own, 4), (count // 2,), 0, 1 << 20) % (margin + 1)
    tallies = tallies.at[giver].add(-moved).at[receiver].add(moved)
    labels = jnp.searchsorted(jnp.cumsum(tallies), jnp.arange(rows * top), side="right").astype(jnp.int32)
    grid = labels.reshape(top, rows).T
    grid = grid[jax.random.permutation(jax.random.fold_in(own, 1), rows)]
    rotation = jax.random.randint(jax.random.fold_in(own, 2), (rows, 1), 0, top)
    return jnp.take_along_axis(grid, (jnp.arange(top)[None, :] + rotation) % top, axis=1)


def portions_of(amount, total, most, slope, full):
    loads = [(1 << 20) // math.isqrt(standing ** slope) + 1 for standing in range(1, amount + 1)]
    largest = most if full else min(most, max(-(-total // amount), total * loads[0] // sum(loads)))
    least = 1 if total - largest >= amount - 1 else 0
    given, rest = [largest] + [least] * (amount - 1), total - largest - least * (amount - 1)
    while rest > 0:
        movable = [i for i in range(1, amount) if given[i] < largest] or [i for i in range(1, amount) if given[i] < most]
        mass, left = sum([loads[i] for i in movable]), rest
        for i in movable:
            extra = min(most - given[i], max(1, left * loads[i] // mass), rest)
            given[i] = given[i] + extra
            rest = rest - extra
    return np.array(given)


def centred(stream_key, dims, deviation, limit, split=(), kind=jnp.bfloat16):
    result = jax.random.normal(stream_key, dims, jnp.float32) * deviation
    if len(split) > 0:
        result = level_of(stream_key, dims, split, -0.22, 0.18) * result
    return jnp.clip(result, min=-limit, max=limit).astype(kind)


def setup_inputs(seed: int = 0) -> dict:
    splits = jax.random.split(jax.random.key(seed), 8)
    tokens = centred(splits[0], (TOKENS, D), 1.0, 6.0, ((0, 256),))
    routes_keys = jax.random.split(jax.random.fold_in(splits[1], 1), TOKENS // TOK_DEV)
    routes_turns = jax.random.permutation(jax.random.fold_in(splits[1], 3), TOKENS // TOK_DEV)
    routes = jax.vmap(lambda own, number: assign_block(jax.random.fold_in(splits[1], 2), own, number, TOK_DEV, EXPERTS, TOP, CAP, 2))(routes_keys, routes_turns).reshape((TOKENS, TOP))
    gates = jnp.clip(jnp.exp(math.log(0.3) - 2.7080503 * jax.random.uniform(splits[2], (TOKENS, TOP), jnp.float32) ** level_of(splits[2], (TOKENS, TOP), ((0, 256),), -0.2, 0.2)), 0.02, 0.3)
    cotangent = centred(splits[3], (TOKENS, D), 1.0, 6.0, ((0, 256),))
    w_gate = centred(splits[4], (EXPERTS, D, H), D ** -0.5, 0.1875, ((0, 16), (1, 16)))
    w_up = centred(splits[5], (EXPERTS, D, H), D ** -0.5, 0.1875, ((0, 16), (1, 16)))
    w_down = centred(splits[6], (EXPERTS, H, D), H ** -0.5, 0.3125, ((0, 16), (2, 16)))
    return dict(tokens=tokens, routes=routes, gates=gates, cotangent=cotangent, w_gate=w_gate, w_up=w_up, w_down=w_down)


def expert_pass(operands):
    received, incoming, gate_weight, up_weight, down_weight = operands
    gate_linear = jnp.dot(received, gate_weight, preferred_element_type=jnp.float32)
    up_linear = jnp.dot(received, up_weight, preferred_element_type=jnp.float32)
    sigmoid_gate = jax.nn.sigmoid(gate_linear)
    hidden = (gate_linear * sigmoid_gate * up_linear).astype(jnp.bfloat16)
    output = jnp.dot(hidden, down_weight, preferred_element_type=jnp.float32).astype(jnp.bfloat16)
    hidden_grad = jnp.dot(incoming, down_weight.T, preferred_element_type=jnp.float32)
    up_grad = (hidden_grad * gate_linear * sigmoid_gate).astype(jnp.bfloat16)
    gate_grad = (hidden_grad * up_linear * sigmoid_gate * (1.0 + gate_linear * (1.0 - sigmoid_gate))).astype(jnp.bfloat16)
    route_grad = (jnp.dot(gate_grad, gate_weight.T, preferred_element_type=jnp.float32)
                  + jnp.dot(up_grad, up_weight.T, preferred_element_type=jnp.float32)).astype(jnp.bfloat16)
    grad_gate_part = jnp.dot(received.T, gate_grad, preferred_element_type=jnp.float32)
    grad_up_part = jnp.dot(received.T, up_grad, preferred_element_type=jnp.float32)
    grad_down_part = jnp.dot(hidden.T, incoming, preferred_element_type=jnp.float32)
    return output, route_grad, grad_gate_part, grad_up_part, grad_down_part


def reference(tokens, routes, gates, cotangent, w_gate, w_up, w_down):
    group_rows = N_EXPERT * TOK_DEV
    slot_total = N_EXPERT * CAP

    def group_step(carry, operands):
        group_tokens, group_routes, group_gates, group_cot = operands
        flat_routes = group_routes.reshape(-1)
        onehot = (flat_routes[:, None] == jnp.arange(EXPERTS, dtype=jnp.int32)[None, :]).astype(jnp.int32)
        slot_rank = jnp.sum((jnp.cumsum(onehot, axis=0) - 1) * onehot, axis=1).astype(jnp.int32)
        slot_index = (flat_routes * slot_total + slot_rank).astype(jnp.int32)
        blank_rows = jnp.zeros((EXPERTS * slot_total, D), jnp.bfloat16)
        token_rows = blank_rows.at[slot_index].set(jnp.repeat(group_tokens, TOP, axis=0))
        scaled = (group_gates[:, :, None] * group_cot[:, None, :].astype(jnp.float32)).astype(jnp.bfloat16)
        scaled_rows = blank_rows.at[slot_index].set(scaled.reshape(-1, D))
        output, route_grad, part_gate, part_up, part_down = lax.map(
            expert_pass,
            (token_rows.reshape(EXPERTS, slot_total, D), scaled_rows.reshape(EXPERTS, slot_total, D), w_gate, w_up, w_down))
        routed = output.reshape(-1, D)[slot_index].reshape(group_rows, TOP, D).astype(jnp.float32)
        mixed = jnp.sum(group_gates[:, :, None] * routed, axis=1).astype(jnp.bfloat16)
        gate_grads = jnp.sum(routed * group_cot[:, None, :].astype(jnp.float32), axis=2)
        back_rows = route_grad.reshape(-1, D)[slot_index].reshape(group_rows, TOP, D).astype(jnp.float32)
        input_grad = jnp.sum(back_rows, axis=1).astype(jnp.bfloat16)
        sum_gate, sum_up, sum_down = carry
        sum_gate = sum_gate + lax.optimization_barrier(part_gate.astype(jnp.bfloat16)).astype(jnp.float32)
        sum_up = sum_up + lax.optimization_barrier(part_up.astype(jnp.bfloat16)).astype(jnp.float32)
        sum_down = sum_down + lax.optimization_barrier(part_down.astype(jnp.bfloat16)).astype(jnp.float32)
        return (sum_gate, sum_up, sum_down), (mixed, input_grad, gate_grads)

    start = (jnp.zeros((EXPERTS, D, H), jnp.float32), jnp.zeros((EXPERTS, D, H), jnp.float32),
             jnp.zeros((EXPERTS, H, D), jnp.float32))
    operands = (tokens.reshape(N_DP, group_rows, D), routes.reshape(N_DP, group_rows, TOP),
                gates.reshape(N_DP, group_rows, TOP), cotangent.reshape(N_DP, group_rows, D))
    sums, stacked = lax.scan(group_step, start, operands)
    mixed = stacked[0].reshape(TOKENS, D)
    input_grad = stacked[1].reshape(TOKENS, D)
    gate_grads = stacked[2].reshape(TOKENS, TOP)
    return (mixed, input_grad, gate_grads, sums[0], sums[1], sums[2])
```

```python
import jax
import jax.numpy as jnp
from jax import lax
from jax.experimental import pallas as pl
from jax.experimental.pallas import tpu as pltpu
from jax.sharding import PartitionSpec as P

BF16 = jnp.bfloat16
F32 = jnp.float32
D, H, TOK, CAP = 1024, 384, 128, 24
NZ, NY, NX = 8, 4, 4
NE = 4
NP = 8
PAIR_ROWS = 2 * CAP
ROWS = 16 * CAP
WID = 3 * H


def dot_nt(a, b):
    return lax.dot_general(a, b, (((1,), (1,)), ((), ())), preferred_element_type=F32)


def dot_tn(a, b):
    return lax.dot_general(a, b, (((0,), (0,)), ((), ())), preferred_element_type=F32)


def dot_nn(a, b):
    return lax.dot_general(a, b, (((1,), (0,)), ((), ())), preferred_element_type=F32)


class Copies:
    def __init__(self, send_sems, recv_sems):
        self.send_sems, self.recv_sems, self.used, self.sent = send_sems, recv_sems, 0, []

    def make(self, src, dst, dev):
        k = self.used
        self.used += 1
        copy = pltpu.make_async_remote_copy(
            src_ref=src,
            dst_ref=dst,
            send_sem=self.send_sems.at[k],
            recv_sem=self.recv_sems.at[k],
            device_id=dev,
            device_id_type=pl.DeviceIdType.MESH,
        )
        self.sent.append(copy)
        return copy

    def drain(self):
        for copy in self.sent:
            copy.wait_send()
        self.sent = []


def kernel(
    tok_ref, cot_ref, w_ref, meta_ref,
    mixed_ref, igrad_ref, gg_ref, out_gate, out_up, out_down,
    xbuf, cbuf, wbuf, mbuf, slot, gate, onehot, xe, se, orow, rrow, gsend,
    pr, ru1, rd1, ru, rd, a1, a2, tsum, b1, b2,
    send_sems, recv_sems, msend, mrecv, gsem_s, gsem_r, local_sems,
):
    dp, ex = lax.axis_index("dp"), lax.axis_index("expert")
    z, c = lax.div(dp, 2), lax.rem(dp, 2)
    y, x = lax.div(ex, NX), lax.rem(ex, NX)
    sibling = (2 * z + (1 - c), ex)

    def mod(a, n):
        return lax.rem(a + n, n)

    def zdev(o):
        return (2 * mod(z + o, NZ) + c, ex)

    def zpos(o):
        return 2 * mod(z + o, NZ) + c

    def plane(oy, ox):
        return mod(y + oy, NY) * NX + mod(x + ox, NX)

    def plane_dev(oy, ox):
        return (dp, plane(oy, ox))

    barrier = pltpu.get_barrier_semaphore()

    def greet(i, _):
        pl.semaphore_signal(
            barrier, inc=1, device_id=(dp, lax.rem(ex + i, 16)), device_id_type=pl.DeviceIdType.MESH
        )
        return 0

    lax.fori_loop(1, 16, greet, 0)
    for dev in (sibling, zdev(1), zdev(-1)):
        pl.semaphore_signal(barrier, inc=1, device_id=dev, device_id_type=pl.DeviceIdType.MESH)
    pl.semaphore_wait(barrier, 18)

    copies = Copies(send_sems, recv_sems)

    def first_dev(first, o):
        return plane_dev(o, 0) if first == "y" else plane_dev(0, o)

    def second_dev(first, o):
        return plane_dev(0, o) if first == "y" else plane_dev(o, 0)

    def pos(first, a, b):
        return plane(a, b) if first == "y" else plane(b, a)

    half = (pl.ds(0, TOK // 2), pl.ds(TOK // 2, TOK // 2))

    class Gather:
        def __init__(self, src, buf, first):
            self.src, self.buf, self.first = src, buf, first
            self.arrive = {}

        def block(self, a, b):
            return self.src if (a, b) == (0, 0) else self.buf.at[pos(self.first, a, b)]

        def send(self, key, a, b, dev, part=None):
            src, dst = self.block(a, b), self.buf.at[pos(self.first, a, b)]
            if part is not None:
                src, dst = src.at[half[part]], dst.at[half[part]]
            copy = copies.make(src, dst, dev)
            copy.start()
            self.arrive[key] = copy

        def own_first(self):
            self.send("r1p", 0, 0, first_dev(self.first, 1))
            self.send("r1m", 0, 0, first_dev(self.first, -1))

        def second(self, a):
            self.send(("p", a), a, 0, second_dev(self.first, 1))
            self.send(("m", a), a, 0, second_dev(self.first, -1))

        def wait(self, key):
            self.arrive[key].wait_recv()

        def on_first(self):
            self.wait("r1p")
            self.send("r2p", -1, 0, first_dev(self.first, 1), 0)
            self.second(-1)
            self.wait("r1m")
            self.send("r2m", 1, 0, first_dev(self.first, -1), 1)
            self.second(1)

        def on_opposite(self):
            self.wait("r2p")
            self.wait("r2m")
            self.second(2)

        def on_second(self, a):
            self.wait(("p", a))
            self.send(("p2", a), a, -1, second_dev(self.first, 1), 0)
            self.wait(("m", a))
            self.send(("m2", a), a, 1, second_dev(self.first, -1), 1)

        def on_last(self, a):
            self.wait(("p2", a))
            self.wait(("m2", a))

    tg = Gather(tok_ref, xbuf, "x")
    cg = Gather(cot_ref, cbuf, "y")
    wring, wsib = {}, {}

    def wpart(o, h):
        return wbuf.at[pl.ds(2 * h, 2), zpos(o)]

    def wsrc(o, h):
        return w_ref.at[pl.ds(2 * h, 2)] if o == 0 else wpart(o, h)

    def wsend(key, o, h, dev):
        copy = copies.make(wsrc(o, h), wpart(o, h), dev)
        copy.start()
        return copy

    def wup(step, h):
        wring[("u", step, h)] = wsend(None, 1 - step, h, zdev(1))

    def wdown(step, h):
        wring[("d", step, h)] = wsend(None, step - 1, h, zdev(-1))

    def wsibling(o, h):
        wsib[(o, h)] = wsend(None, o, h, sibling)

    def on_ring(step, h):
        if step < 4 or h == 0:
            wring[("u", step, h)].wait_recv()
            if step < 3 or (step == 3 and h == 0):
                wup(step + 1, h)
            wsibling(-step, h)
        if step < 4 or h == 1:
            wring[("d", step, h)].wait_recv()
            if step < 3 or (step == 3 and h == 1):
                wdown(step + 1, h)
            wsibling(step, h)

    tg.own_first()
    cg.own_first()
    for h in range(2):
        wup(1, h)
        wdown(1, h)
    tg.second(0)
    cg.second(0)
    local = [
        pltpu.make_async_copy(tok_ref, xbuf.at[ex], local_sems.at[0]),
        pltpu.make_async_copy(cot_ref, cbuf.at[ex], local_sems.at[1]),
        pltpu.make_async_copy(w_ref, wbuf.at[:, dp], local_sems.at[2]),
        pltpu.make_async_copy(meta_ref, mbuf.at[ex], local_sems.at[3]),
    ]
    for copy in local:
        copy.start()

    def meta_copy(i):
        return pltpu.make_async_remote_copy(
            src_ref=meta_ref,
            dst_ref=mbuf.at[ex],
            send_sem=msend.at[i],
            recv_sem=mrecv.at[i],
            device_id=(dp, lax.rem(ex + i, 16)),
            device_id_type=pl.DeviceIdType.MESH,
        )

    def meta_start(i, _):
        meta_copy(i).start()
        return 0

    lax.fori_loop(1, 16, meta_start, 0)
    wsibling(0, 0)
    wsibling(0, 1)
    on_ring(1, 0)
    tg.on_first()
    cg.on_first()
    on_ring(1, 1)
    tg.on_second(0)
    cg.on_second(0)
    tg.on_opposite()
    cg.on_opposite()
    on_ring(2, 0)
    on_ring(2, 1)

    def meta_wait(i, _):
        meta_copy(i).wait()
        return 0

    lax.fori_loop(1, 16, meta_wait, 0)
    for copy in local:
        copy.wait()

    lower = (
        lax.broadcasted_iota(jnp.int32, (TOK, TOK), 0) < lax.broadcasted_iota(jnp.int32, (TOK, TOK), 1)
    ).astype(F32).astype(BF16)
    for odd in range(2):
        names = mbuf.reshape(NP, 2, 16, TOK)[:, odd, 0:8, :]
        values = mbuf.reshape(NP, 2, 16, TOK)[:, odd, 8:16, :]
        for j in range(NE):
            hit = names == (NE * ex + j).astype(F32)
            member = jnp.max(jnp.where(hit, 1.0, 0.0), axis=1)
            weight = jnp.sum(jnp.where(hit, values, 0.0), axis=1)
            rank = dot_nn(member.astype(BF16), lower)
            slot[j, :, odd * TOK : (odd + 1) * TOK] = jnp.where(
                member > 0.5, rank + float(odd * CAP), -1000.0
            )
            gate[j, :, odd * TOK : (odd + 1) * TOK] = weight

    places = lax.broadcasted_iota(jnp.int32, (PAIR_ROWS, 2 * TOK), 0).astype(F32)

    def build(p, _):
        for j in range(NE):
            row = slot[j, pl.ds(p, 1), :]
            onehot[p, j * PAIR_ROWS : (j + 1) * PAIR_ROWS, :] = jnp.where(
                row == places, 1.0, 0.0
            ).astype(BF16)
        return 0

    lax.fori_loop(0, NP, build, 0)

    for a in (-1, 1):
        tg.on_second(a)
        cg.on_second(a)
    on_ring(3, 0)
    tg.on_second(2)
    cg.on_second(2)
    on_ring(3, 1)
    for a in (0, -1, 1, 2):
        tg.on_last(a)
        cg.on_last(a)

    def select(p, _):
        hot = onehot[p]
        rows = dot_nn(hot, xbuf[pl.ds(2 * p, 2)].reshape(2 * TOK, D)).astype(BF16)
        grads = dot_nn(hot, cbuf[pl.ds(2 * p, 2)].reshape(2 * TOK, D))
        at = pl.ds(pl.multiple_of(p * PAIR_ROWS, 16), PAIR_ROWS)
        for j in range(NE):
            part = slice(j * PAIR_ROWS, (j + 1) * PAIR_ROWS)
            weight = jnp.sum(
                hot[part].astype(F32) * gate[j, pl.ds(p, 1), :], axis=1, keepdims=True
            )
            xe[j, at, :] = rows[part]
            se[j, at, :] = (grads[part] * weight).astype(BF16)
        return 0

    lax.fori_loop(0, NP, select, 0)

    on_ring(4, 0)
    on_ring(4, 1)
    for copy in wsib.values():
        copy.wait_recv()
    copies.drain()

    def expert(j):
        xj, sj = xe[j], se[j]
        gate_up = dot_nn(xj, wbuf[j, :, :, 0 : 2 * H].reshape(D, 2 * H))
        hidden_grad = dot_nn(sj, wbuf[j, :, :, 2 * H : WID].reshape(D, H))
        linear, up = gate_up[:, :H], gate_up[:, H:]
        sig = 1.0 / (1.0 + jnp.exp(-linear))
        hidden = (linear * sig * up).astype(BF16)
        up_grad = (hidden_grad * linear * sig).astype(BF16)
        gate_grad = (hidden_grad * up * sig * (1.0 + linear * (1.0 - sig))).astype(BF16)
        both = jnp.concatenate([gate_grad, up_grad], axis=1)
        for d in range(4):
            cols = slice(256 * d, 256 * d + 256)
            out = dot_nt(hidden, wbuf[j, 4 * d : 4 * d + 4, :, 2 * H : WID].reshape(256, H))
            back = dot_nt(both, wbuf[j, 4 * d : 4 * d + 4, :, 0 : 2 * H].reshape(256, 2 * H))
            at = pl.ds(pl.multiple_of(j * PAIR_ROWS, 16), PAIR_ROWS)
            orow[:, at, cols] = out.astype(BF16).reshape(NP, PAIR_ROWS, 256)
            rrow[:, at, cols] = back.astype(BF16).reshape(NP, PAIR_ROWS, 256)
            wbuf[j, 4 * d : 4 * d + 4, :, 0 : 2 * H] = (
                dot_tn(xj[:, cols], both).astype(BF16).reshape(4, 64, 2 * H)
            )
            wbuf[j, 4 * d : 4 * d + 4, :, 2 * H : WID] = (
                dot_tn(sj[:, cols], hidden).astype(BF16).reshape(4, 64, H)
            )

    grads = wbuf.reshape(NE, NZ, 2, 64, WID)
    pair = {}

    def pair_send(g):
        copy = copies.make(grads.at[pl.ds(2 * g, 2), :, 1 - c], pr.at[pl.ds(2 * g, 2)], sibling)
        copy.start()
        pair[g] = copy

    def add_pair(g):
        pair[g].wait_recv()

        def body(i, _):
            e, q = 2 * g + lax.div(i, NZ), lax.rem(i, NZ)
            pr[e, q] = (pr[e, q].astype(F32) + grads[e, q, c].astype(F32)).astype(BF16)
            return 0

        lax.fori_loop(0, 2 * NZ, body, 0)

    up_c, down_c = {}, {}

    def ring1(g):
        far = mod(z + 4, NZ)
        copy = copies.make(pr.at[2 * g, far], ru1.at[g], zdev(1))
        copy.start()
        up_c[(g, 1)] = copy
        copy = copies.make(pr.at[2 * g + 1, far], rd1.at[g], zdev(-1))
        copy.start()
        down_c[(g, 1)] = copy

    def ring_next(g, step):
        for sign, chain, one, many in ((1, up_c, ru1, ru), (-1, down_c, rd1, rd)):
            at = mod(z + sign * (5 - step), NZ)
            chain[(g, step - 1)].wait_recv()
            if step == 2:
                e = 2 * g if sign == 1 else 2 * g + 1
                pr[e, at] = (pr[e, at].astype(F32) + one[g].astype(F32)).astype(BF16)
            else:
                for i in range(2):
                    e = 2 * g + i
                    pr[e, at] = (pr[e, at].astype(F32) + many[step - 3, e].astype(F32)).astype(BF16)
            copy = copies.make(pr.at[pl.ds(2 * g, 2), at], many.at[step - 2, pl.ds(2 * g, 2)], zdev(sign))
            copy.start()
            chain[(g, step)] = copy

    def ring_end(g):
        up_c[(g, 4)].wait_recv()
        down_c[(g, 4)].wait_recv()
        for e in (2 * g, 2 * g + 1):
            total = pr[e, z].astype(F32) + ru[2, e].astype(F32) + rd[2, e].astype(F32)
            out_gate[e] = total[:, 0:H]
            out_up[e] = total[:, H : 2 * H]
            out_down[e] = total[:, 2 * H : WID]

    def run_group(g):
        def body(j, _):
            expert(j)
            return 0

        lax.fori_loop(2 * g, 2 * g + 2, body, 0)

    run_group(0)
    pair_send(0)
    run_group(1)
    pair_send(1)

    def combine(p, _):
        hot = onehot[p]
        out_rows = orow[p]
        score = dot_nt(out_rows, cbuf[pl.ds(2 * p, 2)].reshape(2 * TOK, D))
        weighted = []
        for j in range(NE):
            part = slice(j * PAIR_ROWS, (j + 1) * PAIR_ROWS)
            mask = hot[part].astype(F32)
            weighted.append((mask * gate[j, pl.ds(p, 1), :]).astype(BF16))
            sums = jnp.sum(mask * score[part], axis=0, keepdims=True)
            for odd in range(2):
                gsend[2 * p + odd, j : j + 1, :] = sums[:, odd * TOK : (odd + 1) * TOK]
        mix = dot_tn(jnp.concatenate(weighted, axis=0), out_rows)
        xbuf[pl.ds(2 * p, 2)] = mix.astype(BF16).reshape(2, TOK, D)
        back = dot_tn(hot, rrow[p])
        cbuf[pl.ds(2 * p, 2)] = back.astype(BF16).reshape(2, TOK, D)
        return 0

    gsend[...] = jnp.zeros_like(gsend)
    add_pair(0)
    ring1(0)
    lax.fori_loop(0, NP, combine, 0)

    def gg_copy(i):
        return pltpu.make_async_remote_copy(
            src_ref=gsend.at[lax.rem(ex + i, 16)],
            dst_ref=gg_ref.at[ex],
            send_sem=gsem_s.at[i],
            recv_sem=gsem_r.at[i],
            device_id=(dp, lax.rem(ex + i, 16)),
            device_id_type=pl.DeviceIdType.MESH,
        )

    def gg_start(i, _):
        gg_copy(i).start()
        return 0

    class Scatter:
        def __init__(self, n, buf, out, first):
            self.n, self.out, self.first = n, out, first
            self.buf = buf.reshape(NY, NX, TOK, D)
            self.arrive = {}

        def group(self, o, lo, count):
            if self.first == "y":
                return self.buf.at[mod(y + o, NY), pl.ds(lo, count)]
            return self.buf.at[pl.ds(lo, count), mod(x + o, NX)]

        def send(self, key, src, dst, dev):
            copy = copies.make(src, dst, dev)
            copy.start()
            self.arrive[key] = copy

        def start(self):
            n = self.n
            up, down = first_dev(self.first, 1), first_dev(self.first, -1)
            self.send("a1p", self.group(2, 0, 2), a1.at[n, 0], up)
            self.send("a1m", self.group(2, 2, 2), a1.at[n, 1], down)
            self.send("a2p1", self.group(1, 2, 2), a2.at[n, 0, pl.ds(2, 2)], up)
            self.send("a2m0", self.group(-1, 0, 2), a2.at[n, 1, pl.ds(0, 2)], down)

        def add_first(self, o, lo, k):
            ref = self.group(o, lo, 2)

            def body(i, _):
                b, r = lax.div(i, 2), pl.multiple_of(lax.rem(i, 2) * 64, 64)
                rows = pl.ds(r, 64)
                ref[b, rows] = (
                    ref[b, rows].astype(F32) + a1[self.n, k, b, rows].astype(F32)
                ).astype(BF16)
                return 0

            lax.fori_loop(0, 4, body, 0)

        def middle(self):
            n = self.n
            self.arrive["a1p"].wait_recv()
            self.add_first(1, 0, 0)
            self.send("a2p0", self.group(1, 0, 2), a2.at[n, 0, pl.ds(0, 2)], first_dev(self.first, 1))
            self.arrive["a1m"].wait_recv()
            self.add_first(-1, 2, 1)
            self.send("a2m1", self.group(-1, 2, 2), a2.at[n, 1, pl.ds(2, 2)], first_dev(self.first, -1))

        def sum_own(self):
            for key in ("a2p1", "a2m0", "a2p0", "a2m1"):
                self.arrive[key].wait_recv()
            own = self.group(0, 0, 4)

            def body(i, _):
                b, r = lax.div(i, 2), pl.multiple_of(lax.rem(i, 2) * 64, 64)
                rows = pl.ds(r, 64)
                tsum[self.n, b, rows] = (
                    own[b, rows].astype(F32)
                    + a2[self.n, 0, b, rows].astype(F32)
                    + a2[self.n, 1, b, rows].astype(F32)
                ).astype(BF16)
                return 0

            lax.fori_loop(0, 8, body, 0)

        def at(self, o):
            return mod((x if self.first == "y" else y) + o, 4)

        def second(self):
            n = self.n
            self.sum_own()
            up, down = second_dev(self.first, 1), second_dev(self.first, -1)
            t = tsum.at[n]
            self.send("b1p", t.at[self.at(2), half[0]], b1.at[n, 0], up)
            self.send("b1m", t.at[self.at(2), half[1]], b1.at[n, 1], down)
            self.send("b2p1", t.at[self.at(1), half[1]], b2.at[n, 0, half[1]], up)
            self.send("b2m0", t.at[self.at(-1), half[0]], b2.at[n, 1, half[0]], down)

        def third(self):
            n = self.n
            t = tsum.at[n]
            up, down = second_dev(self.first, 1), second_dev(self.first, -1)
            for key, o, part, k, dev in (("b1p", 1, 0, 0, up), ("b1m", -1, 1, 1, down)):
                self.arrive[key].wait_recv()
                rows, q = half[part], self.at(o)
                t[q, rows] = (t[q, rows].astype(F32) + b1[n, k].astype(F32)).astype(BF16)
                self.send(("b2", k), t.at[q, rows], b2.at[n, k, rows], dev)

        def finish(self):
            for key in ("b2p1", "b2m0", ("b2", 0), ("b2", 1)):
                self.arrive[key].wait_recv()
            n, q = self.n, self.at(0)
            for rows in half:
                self.out[rows] = (
                    tsum[n, q, rows].astype(F32)
                    + b2[n, 0, rows].astype(F32)
                    + b2[n, 1, rows].astype(F32)
                ).astype(BF16)

    ms = Scatter(0, xbuf, mixed_ref, "y")
    gs = Scatter(1, cbuf, igrad_ref, "x")
    ms.start()
    gs.start()
    lax.fori_loop(1, 16, gg_start, 0)
    gg_own = pltpu.make_async_copy(gsend.at[ex], gg_ref.at[ex], local_sems.at[4])
    gg_own.start()
    add_pair(1)
    ring1(1)
    ring_next(0, 2)
    ms.middle()
    gs.middle()
    ring_next(1, 2)
    ring_next(0, 3)
    ring_next(1, 3)
    ms.second()
    gs.second()
    ring_next(0, 4)
    ms.third()
    gs.third()
    ring_next(1, 4)
    ms.finish()
    gs.finish()
    ring_end(0)
    ring_end(1)

    def gg_wait(i, _):
        gg_copy(i).wait()
        return 0

    lax.fori_loop(1, 16, gg_wait, 0)
    gg_own.wait()
    copies.drain()


def step(tokens, cotangent, weights, meta):
    any_spec = pl.BlockSpec(memory_space=pl.ANY)
    vmem = pl.BlockSpec(memory_space=pltpu.VMEM)
    n_copies = 40 + 30 + 2 + 16 + 24
    out = jax.ShapeDtypeStruct
    return pl.pallas_call(
        kernel,
        out_shape=(
            out((TOK, D), BF16),
            out((TOK, D), BF16),
            out((16, 8, TOK), F32),
            out((NE, 64, H), F32),
            out((NE, 64, H), F32),
            out((NE, 64, H), F32),
        ),
        in_specs=[any_spec] * 4,
        out_specs=(vmem,) * 6,
        scratch_shapes=[
            pltpu.VMEM((16, TOK, D), BF16),
            pltpu.VMEM((16, TOK, D), BF16),
            pltpu.VMEM((NE, 16, 64, WID), BF16),
            pltpu.VMEM((16, 16, TOK), F32),
            pltpu.VMEM((NE, NP, 2 * TOK), F32),
            pltpu.VMEM((NE, NP, 2 * TOK), F32),
            pltpu.VMEM((NP, NE * PAIR_ROWS, 2 * TOK), BF16),
            pltpu.VMEM((NE, ROWS, D), BF16),
            pltpu.VMEM((NE, ROWS, D), BF16),
            pltpu.VMEM((NP, NE * PAIR_ROWS, D), BF16),
            pltpu.VMEM((NP, NE * PAIR_ROWS, D), BF16),
            pltpu.VMEM((16, 8, TOK), F32),
            pltpu.VMEM((NE, NZ, 64, WID), BF16),
            pltpu.VMEM((2, 64, WID), BF16),
            pltpu.VMEM((2, 64, WID), BF16),
            pltpu.VMEM((3, NE, 64, WID), BF16),
            pltpu.VMEM((3, NE, 64, WID), BF16),
            pltpu.VMEM((2, 2, 2, TOK, D), BF16),
            pltpu.VMEM((2, 2, 4, TOK, D), BF16),
            pltpu.VMEM((2, 4, TOK, D), BF16),
            pltpu.VMEM((2, 2, TOK // 2, D), BF16),
            pltpu.VMEM((2, 2, TOK, D), BF16),
            pltpu.SemaphoreType.DMA((n_copies,)),
            pltpu.SemaphoreType.DMA((n_copies,)),
            pltpu.SemaphoreType.DMA((16,)),
            pltpu.SemaphoreType.DMA((16,)),
            pltpu.SemaphoreType.DMA((16,)),
            pltpu.SemaphoreType.DMA((16,)),
            pltpu.SemaphoreType.DMA((5,)),
        ],
        compiler_params=pltpu.CompilerParams(
            collective_id=0, has_side_effects=True, vmem_limit_bytes=63 * 1024 * 1024
        ),
    )(tokens, cotangent, weights, meta)


def body(tokens, routes, gates, cotangent, w_gate, w_up, w_down):
    meta = jnp.concatenate([routes.T.astype(F32), gates.T], axis=0)
    weights = jnp.concatenate([w_gate, w_up, jnp.swapaxes(w_down, 1, 2)], axis=2)
    mixed, igrad, by_expert, grad_gate, grad_up, grad_down = step(tokens, cotangent, weights, meta)
    table = by_expert[:, :NE, :].reshape(16 * NE, TOK)
    named = routes.T[:, None, :] == jnp.arange(16 * NE, dtype=jnp.int32)[None, :, None]
    gate_grads = jnp.sum(jnp.where(named, table[None], 0.0), axis=1).T
    return (mixed, igrad, gate_grads, grad_gate, grad_up, jnp.swapaxes(grad_down, 1, 2))


def solution(mesh):
    rows = P(("dp", "expert"), None)
    features = P("expert", "dp", None)
    last = P("expert", None, "dp")
    return jax.shard_map(
        body,
        mesh=mesh,
        in_specs=(rows, rows, rows, rows, features, features, last),
        out_specs=(rows, rows, rows, features, features, last),
        check_vma=False,
    )
```

```python
import jax
import jax.numpy as jnp
from jax import lax
from jax.experimental import pallas as pl
from jax.experimental.pallas import tpu as pltpu
from jax.sharding import PartitionSpec as P

BF16 = jnp.bfloat16
F32 = jnp.float32
D, H, TOK, CAP = 1024, 384, 128, 24
NZ, NY, NX = 8, 4, 4
NE = 4
NP = 8
PAIR_ROWS = 2 * CAP
ROWS = 16 * CAP
WID = 3 * H
PART = TOK // 2
MESH = pl.DeviceIdType.MESH
OFFSETS = (0, -1, 1, 2)

(
    OWN,
    FORTH,
    BACK,
    FAR,
    PLUS,
    MINUS,
    W_OWN,
    W_UP,
    W_DOWN,
    W_FAR,
    META,
    SELECT_X,
    SELECT_C,
    FWD,
    BWD_A,
    BWD_B,
    PAIR_A,
    PAIR_B,
    RING_UP,
    RING_DOWN,
    RING_END,
    SUM_UP,
    SUM_DOWN,
    SUM_OWN,
    LAST_UP,
    LAST_DOWN,
    LAST,
    MIX,
    IGRAD,
    TURN,
) = range(30)
TA, TB, CA, CB = range(4)

ORDER = (
    (OWN, TB), (OWN, TA), (W_OWN, 1), (W_OWN, 3), (MINUS, TB, 0), (W_UP, 1, 1), (FORTH, TB),
    (OWN, CA), (W_OWN, 0), (BACK, TB), (BACK, TA), (W_DOWN, 3, 1), (FAR, TB), (W_DOWN, 0, 1),
    (W_UP, 3, 1), (OWN, CB), (PLUS, TA, 0), (FORTH, TA), (W_OWN, 2), (W_DOWN, 3, 2),
    (MINUS, TA, 0), (W_UP, 0, 1), (W_DOWN, 0, 2), (FORTH, CB), (PLUS, TB, 0), (MINUS, CA, 0),
    (W_DOWN, 1, 1), (MINUS, TB, 1), (W_UP, 3, 2), (BACK, CA), (FAR, TA), (BACK, CB), (FORTH, CA),
    (PLUS, TB, 2), (PLUS, TA, 1), (W_UP, 0, 2), (MINUS, CB, 1), (MINUS, TA, 1), (PLUS, TB, 3),
    (MINUS, TB, 2), (PLUS, TA, 3), (W_DOWN, 0, 3), (W_UP, 3, 3), (MINUS, TB, 3), (W_UP, 2, 1),
    (W_DOWN, 3, 3), (PLUS, TB, 1), (FAR, CB), (W_DOWN, 2, 1), (PLUS, CB, 0), (W_DOWN, 1, 2),
    (MINUS, TA, 3), (W_UP, 0, 3), (PLUS, TA, 2), (MINUS, TA, 2), (FAR, CA), (PLUS, CA, 2),
    (MINUS, CB, 0), (PLUS, CB, 1), (W_FAR, 3), (W_UP, 1, 2), (MINUS, CA, 2), (PLUS, CB, 2),
    (W_UP, 2, 2), (META,), (W_DOWN, 2, 2), (PLUS, CA, 0), (SELECT_X,), (MINUS, CB, 2), (W_FAR, 0),
    (PLUS, CB, 3), (MINUS, CA, 1), (PLUS, CA, 3), (FWD, 3), (MINUS, CB, 3), (W_UP, 1, 3),
    (PLUS, CA, 1), (W_DOWN, 1, 3), (MINUS, CA, 3), (TURN,), (FWD, 0), (W_DOWN, 2, 3), (W_UP, 2, 3),
    (SELECT_C,), (W_FAR, 1), (BWD_A, 0), (W_FAR, 2), (BWD_A, 3), (BWD_B, 0), (BWD_B, 3), (FWD, 1),
    (PAIR_A, 0), (FWD, 2), (PAIR_A, 3), (MIX,), (PAIR_B, 0), (RING_UP, 0, 1), (RING_DOWN, 0, 1),
    (BWD_A, 2), (BWD_B, 2), (PAIR_B, 3), (RING_DOWN, 3, 1), (RING_UP, 3, 1), (BWD_A, 1),
    (BWD_B, 1), (RING_DOWN, 0, 2), (RING_UP, 0, 2), (PAIR_A, 2), (RING_DOWN, 3, 2),
    (RING_UP, 3, 2), (IGRAD,), (PAIR_B, 1), (RING_UP, 0, 3), (SUM_UP, TB), (RING_DOWN, 0, 3),
    (PAIR_B, 2), (SUM_DOWN, TA), (RING_UP, 3, 3), (RING_DOWN, 3, 3), (SUM_DOWN, TB), (PAIR_A, 1),
    (SUM_UP, TA), (SUM_UP, CB), (RING_UP, 2, 1), (SUM_UP, CA), (SUM_DOWN, CA), (RING_DOWN, 2, 1),
    (RING_END, 0), (RING_END, 3), (RING_UP, 1, 1), (RING_DOWN, 1, 1), (RING_DOWN, 2, 2),
    (RING_UP, 2, 2), (SUM_DOWN, CB), (SUM_OWN, TB), (RING_DOWN, 1, 2), (RING_UP, 1, 2),
    (SUM_OWN, TA), (RING_UP, 2, 3), (RING_DOWN, 2, 3), (SUM_OWN, CA), (SUM_OWN, CB), (LAST_UP, TA),
    (RING_UP, 1, 3), (LAST_UP, TB), (RING_DOWN, 1, 3), (LAST_DOWN, TB), (LAST_DOWN, TA),
    (LAST_DOWN, CA), (LAST_UP, CA), (LAST_DOWN, CB), (RING_END, 2), (LAST_UP, CB), (LAST, TB),
    (LAST, TA), (RING_END, 1), (LAST, CB), (LAST, CA),
)


def dot_nt(a, b):
    return lax.dot_general(a, b, (((1,), (1,)), ((), ())), preferred_element_type=F32)


def dot_tn(a, b):
    return lax.dot_general(a, b, (((0,), (0,)), ((), ())), preferred_element_type=F32)


def dot_nn(a, b):
    return lax.dot_general(a, b, (((1,), (0,)), ((), ())), preferred_element_type=F32)


def kernel(
    tok_ref, cot_ref, wg_ref, wu_ref, wd_ref, routes_ref, gates_ref,
    mixed_ref, igrad_ref, gg_ref, out_gate, out_up, out_down,
    xbuf, cbuf, wbuf, mbuf, slot, gate, onehot, weighted, hot_t, weighted_t, xe, se, lin, hid, both_ref, orow, rrow, gsend, grecv,
    pr, ru1, rd1, ru, rd, a1, a2, b1, b2, fout, gout,
    send_sems, recv_sems, msend, mrecv, gsem_s, gsem_r, local_sems, out_sems,
):
    dp, ex = lax.axis_index("dp"), lax.axis_index("expert")
    z, c = lax.div(dp, 2), lax.rem(dp, 2)
    y, x = lax.div(ex, NX), lax.rem(ex, NX)
    sibling = (2 * z + (1 - c), ex)

    def mod(a, n):
        return lax.rem(a + n, n)

    def zdev(o):
        return (2 * mod(z + o, NZ) + c, ex)

    def zpos(o):
        return 2 * mod(z + o, NZ) + c

    def plane(oy, ox):
        return mod(y + oy, NY) * NX + mod(x + ox, NX)

    def plane_dev(oy, ox):
        return (dp, plane(oy, ox))

    barrier = pltpu.get_barrier_semaphore()

    def greet(i, _):
        pl.semaphore_signal(barrier, inc=1, device_id=(dp, lax.rem(ex + i, 16)), device_id_type=MESH)
        return 0

    lax.fori_loop(1, 16, greet, 0)
    for dev in (sibling, zdev(1), zdev(-1)):
        pl.semaphore_signal(barrier, inc=1, device_id=dev, device_id_type=MESH)
    local = [
        pltpu.make_async_copy(tok_ref, xbuf.at[ex], local_sems.at[0]),
        pltpu.make_async_copy(cot_ref, cbuf.at[ex], local_sems.at[1]),
        pltpu.make_async_copy(wg_ref, wbuf.at[:, dp, :, pl.ds(0, H)], local_sems.at[2]),
        pltpu.make_async_copy(wu_ref, wbuf.at[:, dp, :, pl.ds(H, H)], local_sems.at[2]),
        pltpu.make_async_copy(wd_ref, wbuf.at[:, dp, :, pl.ds(2 * H, H)], local_sems.at[2]),
    ]
    for copy in local:
        copy.start()
    mbuf[ex, 0:8, :] = routes_ref[...].astype(F32)
    mbuf[ex, 8:16, :] = gates_ref[...]
    gsend[...] = jnp.zeros_like(gsend)
    pl.semaphore_wait(barrier, 18)

    arrivals, departures, pending, actions = {}, {}, {}, {}

    def send(key, src, dst, dev, group):
        copy = pltpu.make_async_remote_copy(
            src_ref=src,
            dst_ref=dst,
            send_sem=send_sems.at[departures.setdefault(group, len(departures))],
            recv_sem=recv_sems.at[arrivals.setdefault(key, len(arrivals))],
            device_id=dev,
            device_id_type=MESH,
        )
        copy.start()
        pending[key] = copy

    def wait(*key):
        pending.pop(key).wait_recv()

    def wait_all(ref, *key):
        pltpu.make_async_copy(ref, ref, recv_sems.at[arrivals[key]]).wait()

    def drain(ref, group):
        pltpu.make_async_copy(ref, ref, send_sems.at[departures[group]]).wait()

    def plane_axes(first):
        if first == "y":
            return (lambda o: plane_dev(o, 0)), (lambda o: plane_dev(0, o)), plane
        return (lambda o: plane_dev(0, o)), (lambda o: plane_dev(o, 0)), (lambda a, b: plane(b, a))

    def gather(n, group, arg, buf, first, lo):
        dev1, dev2, pos = plane_axes(first)
        halves = (pl.ds(lo, PART // 2), pl.ds(lo + PART // 2, PART // 2))

        def move(key, a, b, dev, rows):
            ref = buf.at[pos(a, b), rows]
            send((n,) + key, arg.at[rows] if (a, b) == (0, 0) else ref, ref, dev, group)

        whole = pl.ds(lo, PART)

        def second(i):
            move(("p", i), OFFSETS[i], 0, dev2(1), whole)
            move(("m", i), OFFSETS[i], 0, dev2(-1), whole)

        def own():
            move(("r1p",), 0, 0, dev1(1), whole)
            move(("r1m",), 0, 0, dev1(-1), whole)
            second(0)

        def forward():
            wait(n, "r1p")
            move(("r2",), -1, 0, dev1(1), halves[0])
            second(1)

        def backward():
            wait(n, "r1m")
            move(("r2",), 1, 0, dev1(-1), halves[1])
            second(2)

        def opposite():
            wait_all(buf.at[0, whole], n, "r2")
            second(3)

        def plus(i):
            wait(n, "p", i)
            move(("last",), OFFSETS[i], -1, dev2(1), halves[0])

        def minus(i):
            wait(n, "m", i)
            move(("last",), OFFSETS[i], 1, dev2(-1), halves[1])

        actions[OWN, n] = own
        actions[FORTH, n] = forward
        actions[BACK, n] = backward
        actions[FAR, n] = opposite
        for i in range(4):
            actions[PLUS, n, i] = lambda i=i: plus(i)
            actions[MINUS, n, i] = lambda i=i: minus(i)

    gather(TA, "t", tok_ref, xbuf, "x", 0)
    gather(TB, "t", tok_ref, xbuf, "y", PART)
    gather(CA, "c", cot_ref, cbuf, "x", 0)
    gather(CB, "c", cot_ref, cbuf, "y", PART)

    def gathered(arrays, copy, buf):
        copy.wait()
        for n in arrays:
            wait_all(buf.at[pl.ds(0, 4), pl.ds(0, PART)], n, "last")

    own_weights = [wbuf.at[:, dp]]

    def weight(e):
        def move(key, o, dev, rows=None):
            ref = wbuf.at[e, zpos(o)]
            if rows is not None:
                ref = ref.at[rows]
            send(("w", e) + key, ref, ref, dev, ("w", e))

        def own():
            if own_weights:
                pltpu.make_async_copy(own_weights[0], own_weights.pop(), local_sems.at[2]).wait()
            move(("u", 1), 0, zdev(1))
            move(("d", 1), 0, zdev(-1))
            move(("s",), 0, sibling)

        def up(k):
            wait("w", e, "u", k)
            move(("far",) if k == 3 else ("u", k + 1), -k, zdev(1), pl.ds(0, 32) if k == 3 else None)
            move(("s",), -k, sibling)

        def down(k):
            wait("w", e, "d", k)
            move(("far",) if k == 3 else ("d", k + 1), k, zdev(-1), pl.ds(32, 32) if k == 3 else None)
            move(("s",), k, sibling)

        def opposite():
            wait_all(wbuf.at[e, 0], "w", e, "far")
            move(("s",), 4, sibling)

        actions[W_OWN, e] = own
        actions[W_FAR, e] = opposite
        for k in (1, 2, 3):
            actions[W_UP, e, k] = lambda k=k: up(k)
            actions[W_DOWN, e, k] = lambda k=k: down(k)

    for e in range(NE):
        weight(e)

    def meta_copy(i):
        return pltpu.make_async_remote_copy(
            src_ref=mbuf.at[ex],
            dst_ref=mbuf.at[ex],
            send_sem=msend,
            recv_sem=mrecv,
            device_id=(dp, lax.rem(ex + i, 16)),
            device_id_type=MESH,
        )

    def meta_start(i, _):
        meta_copy(i).start()
        return 0

    def meta():
        for sem in (msend, mrecv):
            pltpu.make_async_copy(mbuf.at[pl.ds(0, 15)], mbuf.at[pl.ds(0, 15)], sem).wait()
        lower = (
            lax.broadcasted_iota(jnp.int32, (TOK, TOK), 0)
            < lax.broadcasted_iota(jnp.int32, (TOK, TOK), 1)
        ).astype(F32).astype(BF16)
        paired = mbuf.reshape(NP, 2, 16, TOK)
        for odd in range(2):
            names = paired[:, odd, 0:8, :]
            values = paired[:, odd, 8:16, :]
            cols = slice(odd * TOK, (odd + 1) * TOK)
            for j in range(NE):
                hit = names == (NE * ex + j).astype(F32)
                member = jnp.max(jnp.where(hit, 1.0, 0.0), axis=1)
                rank = dot_nn(member.astype(BF16), lower)
                slot[j, :, cols] = jnp.where(member > 0.5, rank + float(odd * CAP), -1000.0)
                gate[j, :, cols] = jnp.sum(jnp.where(hit, values, 0.0), axis=1)
        places = lax.broadcasted_iota(jnp.int32, (PAIR_ROWS, 2 * TOK), 0).astype(F32)

        def build(p, _):
            for j in range(NE):
                part = slice(j * PAIR_ROWS, (j + 1) * PAIR_ROWS)
                hit = slot[j, pl.ds(p, 1), :] == places
                onehot[p, part, :] = jnp.where(hit, 1.0, 0.0).astype(BF16)
                weighted[p, part, :] = jnp.where(hit, gate[j, pl.ds(p, 1), :], 0.0).astype(BF16)
            return 0

        lax.fori_loop(0, NP, build, 0)

    actions[(META,)] = meta

    def turn():
        def body(p, _):
            hot_t[p] = onehot[p].T
            weighted_t[p] = weighted[p].T
            return 0

        lax.fori_loop(0, NP, body, 0)

    actions[(TURN,)] = turn

    def pair_at(p):
        return pl.ds(pl.multiple_of(p * PAIR_ROWS, 16), PAIR_ROWS)

    def select_tokens():
        gathered((TA, TB), local[0], xbuf)

        def body(p, _):
            rows = dot_nn(onehot[p], xbuf[pl.ds(2 * p, 2)].reshape(2 * TOK, D)).astype(BF16)
            for j in range(NE):
                xe[j, pair_at(p), :] = rows[j * PAIR_ROWS : (j + 1) * PAIR_ROWS]
            return 0

        lax.fori_loop(0, NP, body, 0, unroll=4)

    def select_cotangent():
        gathered((CA, CB), local[1], cbuf)

        def body(p, _):
            rows = dot_nn(weighted[p], cbuf[pl.ds(2 * p, 2)].reshape(2 * TOK, D)).astype(BF16)
            for j in range(NE):
                se[j, pair_at(p), :] = rows[j * PAIR_ROWS : (j + 1) * PAIR_ROWS]
            return 0

        lax.fori_loop(0, NP, body, 0, unroll=4)

    actions[(SELECT_X,)] = select_tokens
    actions[(SELECT_C,)] = select_cotangent

    def forward(e):
        wait_all(wbuf.at[e, pl.ds(0, 8)], "w", e, "s")
        gate_up = dot_nn(xe[e], wbuf[e, :, :, 0 : 2 * H].reshape(D, 2 * H))
        lin[e] = gate_up
        linear, up = gate_up[:, :H], gate_up[:, H:]
        sig = 1.0 / (1.0 + jnp.exp(-linear))
        hidden = (linear * sig * up).astype(BF16)
        hid[e] = hidden
        out = dot_nt(hidden, wbuf[e, :, :, 2 * H : WID].reshape(D, H))
        orow[:, e * PAIR_ROWS : (e + 1) * PAIR_ROWS, :] = out.astype(BF16).reshape(NP, PAIR_ROWS, D)

    grads = wbuf.reshape(NE, NZ, 2, 64, WID)
    far = 1 - lax.div(z, 4)

    def half_z(o):
        return 4 * lax.rem(far + o, 2)

    def half_grads(e, o):
        q = lax.rem(far + o, 2)
        blocks, cols = pl.ds(8 * q, 8), pl.ds(pl.multiple_of(512 * q, 512), 512)
        both, hidden = both_ref[e], hid[e]
        back = dot_nt(both, wbuf[e, blocks, :, 0 : 2 * H].reshape(512, 2 * H))
        rrow[:, e * PAIR_ROWS : (e + 1) * PAIR_ROWS, cols] = (
            back.astype(BF16).reshape(NP, PAIR_ROWS, 512)
        )
        wbuf[e, blocks, :, 0 : 2 * H] = (
            dot_tn(xe[e, :, cols], both).astype(BF16).reshape(8, 64, 2 * H)
        )
        wbuf[e, blocks, :, 2 * H : WID] = (
            dot_tn(se[e, :, cols], hidden).astype(BF16).reshape(8, 64, H)
        )

    def pair_send(e, o):
        at = half_z(o)
        send(
            ("pair", e, o),
            grads.at[e, pl.ds(at, 4), 1 - c],
            pr.at[e, pl.ds(at, 4)],
            sibling,
            ("z", e),
        )

    def backward_first(e):
        drain(wbuf.at[e, pl.ds(0, 15)], ("w", e))
        hidden_grad = dot_nn(se[e], wbuf[e, :, :, 2 * H : WID].reshape(D, H))
        linear, up = lin[e, :, :H], lin[e, :, H:]
        sig = 1.0 / (1.0 + jnp.exp(-linear))
        up_grad = (hidden_grad * linear * sig).astype(BF16)
        gate_grad = (hidden_grad * up * sig * (1.0 + linear * (1.0 - sig))).astype(BF16)
        products = jnp.sum(hid[e].astype(F32) * hidden_grad, axis=1, keepdims=True)
        for p in range(NP):
            hot = onehot[p, e * PAIR_ROWS : (e + 1) * PAIR_ROWS, :].astype(F32)
            sums = jnp.sum(hot * products[p * PAIR_ROWS : (p + 1) * PAIR_ROWS], axis=0, keepdims=True)
            scale = gate[e, p : p + 1, :].astype(BF16).astype(F32)
            sums = jnp.where(scale > 0.0, sums / jnp.where(scale > 0.0, scale, 1.0), 0.0)
            for odd in range(2):
                gsend[2 * p + odd, e : e + 1, :] = sums[:, odd * TOK : (odd + 1) * TOK]
        both_ref[e, :, :H] = gate_grad
        both_ref[e, :, H:] = up_grad
        half_grads(e, 0)
        pair_send(e, 0)

    def backward_rest(e):
        half_grads(e, 1)
        pair_send(e, 1)

    def add_pair(e, o):
        wait("pair", e, o)
        at = half_z(o)
        for i in range(4):
            pr[e, at + i] = (pr[e, at + i].astype(F32) + grads[e, at + i, c].astype(F32)).astype(BF16)

    def ring_start(e):
        add_pair(e, 0)
        opposite = mod(z + 4, NZ)
        send(("ru", e, 1), pr.at[e, opposite, pl.ds(0, 32)], ru1.at[e], zdev(1), ("z", e))
        send(("rd", e, 1), pr.at[e, opposite, pl.ds(32, 32)], rd1.at[e], zdev(-1), ("z", e))

    def ring_rest(e):
        add_pair(e, 1)

    def ring(e, k, sign):
        name, one, many = ("ru", ru1, ru) if sign == 1 else ("rd", rd1, rd)
        at = mod(z + sign * (4 - k), NZ)
        wait(name, e, k)
        if k == 1:
            rows = pl.ds(0, 32) if sign == 1 else pl.ds(32, 32)
            pr[e, at, rows] = (pr[e, at, rows].astype(F32) + one[e].astype(F32)).astype(BF16)
        else:
            pr[e, at] = (pr[e, at].astype(F32) + many[k - 2, e].astype(F32)).astype(BF16)
        key = ("end", e) if k == 3 else (name, e, k + 1)
        send(key, pr.at[e, at], many.at[k - 1, e], zdev(sign), ("z", e))

    def put(src, dst, k):
        pltpu.make_async_copy(src, dst, out_sems.at[k]).start()

    def ring_end(e):
        wait_all(pr.at[e, pl.ds(0, 2)], "end", e)
        total = pr[e, z].astype(F32) + ru[2, e].astype(F32) + rd[2, e].astype(F32)
        for i, ref in enumerate((out_gate, out_up, out_down)):
            gout[i, e] = total[:, i * H : (i + 1) * H]
            put(gout.at[i, e], ref.at[e], 1)

    for e in range(NE):
        actions[FWD, e] = lambda e=e: forward(e)
        actions[BWD_A, e] = lambda e=e: backward_first(e)
        actions[BWD_B, e] = lambda e=e: backward_rest(e)
        actions[PAIR_A, e] = lambda e=e: ring_start(e)
        actions[PAIR_B, e] = lambda e=e: ring_rest(e)
        actions[RING_END, e] = lambda e=e: ring_end(e)
        for k in (1, 2, 3):
            actions[RING_UP, e, k] = lambda e=e, k=k: ring(e, k, 1)
            actions[RING_DOWN, e, k] = lambda e=e, k=k: ring(e, k, -1)

    def scatter(n, buf, out, first, lo, group_of_sends):
        dev1, dev2, _ = plane_axes(first)
        blocks = buf.reshape(NY, NX, TOK, D)
        whole = pl.ds(lo, PART)
        halves = (pl.ds(lo, PART // 2), pl.ds(lo + PART // 2, PART // 2))
        local_halves = (pl.ds(0, PART // 2), pl.ds(PART // 2, PART // 2))
        mine, other = (y, x) if first == "y" else (x, y)

        def group(o, at, count):
            if first == "y":
                return blocks.at[mod(mine + o, 4), pl.ds(at, count), whole]
            return blocks.at[pl.ds(at, count), mod(mine + o, 4), whole]

        def own(o, rows):
            if first == "y":
                return blocks.at[mine, mod(other + o, 4), rows]
            return blocks.at[mod(other + o, 4), mine, rows]

        def start():
            yield lambda: send((n, "a1p"), group(2, 0, 2), a1.at[n, 0], dev1(1), group_of_sends)
            yield lambda: send((n, "a1m"), group(2, 2, 2), a1.at[n, 1], dev1(-1), group_of_sends)
            yield lambda: send(
                (n, "a2"), group(1, 2, 2), a2.at[n, 0, pl.ds(2, 2)], dev1(1), group_of_sends
            )
            yield lambda: send(
                (n, "a2"), group(-1, 0, 2), a2.at[n, 1, pl.ds(0, 2)], dev1(-1), group_of_sends
            )

        def add(key, k, o, at, name):
            wait(n, key)
            ref = group(o, at, 2)
            for i in range(2):
                ref[i] = (ref[i].astype(F32) + a1[n, k, i].astype(F32)).astype(BF16)
            send((n, name), ref, a2.at[n, k, pl.ds(at, 2)], dev1(o), group_of_sends)

        def total():
            wait_all(a2.at[n], n, "a2")
            for o in (2, 1, -1, 0):
                ref, at = own(o, whole), mod(other + o, 4)
                ref[...] = (
                    ref[...].astype(F32)
                    + a2[n, 0, at].astype(F32)
                    + a2[n, 1, at].astype(F32)
                ).astype(BF16)
                if o == 2:
                    send((n, "b1p"), own(2, halves[0]), b1.at[n, 0], dev2(1), group_of_sends)
                    send((n, "b1m"), own(2, halves[1]), b1.at[n, 1], dev2(-1), group_of_sends)
                if o == 1:
                    send(
                        (n, "b2"), own(1, halves[1]), b2.at[n, 0, local_halves[1]], dev2(1), group_of_sends
                    )
                if o == -1:
                    send(
                        (n, "b2"), own(-1, halves[0]), b2.at[n, 1, local_halves[0]], dev2(-1), group_of_sends
                    )

        def add_second(key, k, o, name):
            wait(n, key)
            ref = own(o, halves[k])
            ref[...] = (ref[...].astype(F32) + b1[n, k].astype(F32)).astype(BF16)
            send((n, name), ref, b2.at[n, k, local_halves[k]], dev2(o), group_of_sends)

        def finish():
            wait_all(b2.at[n], n, "b2")
            fout[n] = (
                own(0, whole)[...].astype(F32)
                + b2[n, 0].astype(F32)
                + b2[n, 1].astype(F32)
            ).astype(BF16)
            put(fout.at[n], out.at[whole], 0)

        actions[SUM_UP, n] = lambda: add("a1p", 0, 1, 0, "a2")
        actions[SUM_DOWN, n] = lambda: add("a1m", 1, -1, 2, "a2")
        actions[SUM_OWN, n] = total
        actions[LAST_UP, n] = lambda: add_second("b1p", 0, 1, "b2")
        actions[LAST_DOWN, n] = lambda: add_second("b1m", 1, -1, "b2")
        actions[LAST, n] = finish
        return start

    starts = {
        "m": (
            scatter(TA, xbuf, mixed_ref, "y", 0, "m"),
            scatter(TB, xbuf, mixed_ref, "x", PART, "m"),
        ),
        "i": (
            scatter(CA, cbuf, igrad_ref, "x", 0, "i"),
            scatter(CB, cbuf, igrad_ref, "y", PART, "i"),
        ),
    }

    def start_sums(n):
        for one, two in zip(starts[n][0](), starts[n][1]()):
            one()
            two()

    def mix():
        drain(xbuf.at[pl.ds(0, 15)], "t")

        def body(p, _):
            mixed = dot_nn(weighted_t[p], orow[p])
            xbuf[pl.ds(2 * p, 2)] = mixed.astype(BF16).reshape(2, TOK, D)
            return 0

        lax.fori_loop(0, NP, body, 0, unroll=4)
        start_sums("m")

    def gg_copy(i):
        return pltpu.make_async_remote_copy(
            src_ref=gsend.at[lax.rem(ex + i, 16)],
            dst_ref=grecv.at[ex],
            send_sem=gsem_s,
            recv_sem=gsem_r,
            device_id=(dp, lax.rem(ex + i, 16)),
            device_id_type=MESH,
        )

    def gg_start(i, _):
        gg_copy(i).start()
        return 0

    def input_grads():
        drain(cbuf.at[pl.ds(0, 15)], "c")

        def body(p, _):
            back = dot_nn(hot_t[p], rrow[p])
            cbuf[pl.ds(2 * p, 2)] = back.astype(BF16).reshape(2, TOK, D)
            return 0

        lax.fori_loop(0, NP, body, 0, unroll=4)
        start_sums("i")
        lax.fori_loop(1, 16, gg_start, 0)

    actions[(MIX,)] = mix
    actions[(IGRAD,)] = input_grads

    lax.fori_loop(1, 16, meta_start, 0)
    for name in ORDER:
        actions[name]()

    for sem in (gsem_s, gsem_r):
        pltpu.make_async_copy(grecv.at[pl.ds(0, 15)], grecv.at[pl.ds(0, 15)], sem).wait()
    grecv[ex] = gsend[ex]
    named = routes_ref[...]
    total = jnp.zeros((8, TOK), F32)
    for owner in range(16):
        for j in range(NE):
            total = total + jnp.where(named == NE * owner + j, grecv[owner, j : j + 1, :], 0.0)
    gg_ref[...] = total
    drain(xbuf.at[pl.ds(0, 15)], "m")
    drain(cbuf.at[pl.ds(0, 15)], "i")
    for e in range(NE):
        drain(wbuf.at[e, pl.ds(0, 15)], ("z", e))
    pltpu.make_async_copy(fout, fout, out_sems.at[0]).wait()
    pltpu.make_async_copy(gout, gout, out_sems.at[1]).wait()


def hand_over(*refs):
    for src, dst in zip(refs[:6], refs[6:]):
        dst[...] = src[...]


def step(tokens, cotangent, w_gate, w_up, w_down, routes, gates):
    any_spec = pl.BlockSpec(memory_space=pl.ANY)
    vmem = pl.BlockSpec(memory_space=pltpu.VMEM)
    out = jax.ShapeDtypeStruct
    shapes = (
        out((TOK, D), BF16),
        out((TOK, D), BF16),
        out((8, TOK), F32),
        out((NE, 64, H), F32),
        out((NE, 64, H), F32),
        out((NE, 64, H), F32),
    )
    mixed, igrad, scores, gate, up, down = pl.pallas_call(
        kernel,
        out_shape=shapes,
        in_specs=[any_spec] * 5 + [vmem] * 2,
        out_specs=(any_spec, any_spec, vmem, any_spec, any_spec, any_spec),
        scratch_shapes=[
            pltpu.VMEM((16, TOK, D), BF16),
            pltpu.VMEM((16, TOK, D), BF16),
            pltpu.VMEM((NE, 16, 64, WID), BF16),
            pltpu.VMEM((16, 16, TOK), F32),
            pltpu.VMEM((NE, NP, 2 * TOK), F32),
            pltpu.VMEM((NE, NP, 2 * TOK), F32),
            pltpu.VMEM((NP, NE * PAIR_ROWS, 2 * TOK), BF16),
            pltpu.VMEM((NP, NE * PAIR_ROWS, 2 * TOK), BF16),
            pltpu.VMEM((NP, 2 * TOK, NE * PAIR_ROWS), BF16),
            pltpu.VMEM((NP, 2 * TOK, NE * PAIR_ROWS), BF16),
            pltpu.VMEM((NE, ROWS, D), BF16),
            pltpu.VMEM((NE, ROWS, D), BF16),
            pltpu.VMEM((NE, ROWS, 2 * H), F32),
            pltpu.VMEM((NE, ROWS, H), BF16),
            pltpu.VMEM((NE, ROWS, 2 * H), BF16),
            pltpu.VMEM((NP, NE * PAIR_ROWS, D), BF16),
            pltpu.VMEM((NP, NE * PAIR_ROWS, D), BF16),
            pltpu.VMEM((16, 8, TOK), F32),
            pltpu.VMEM((16, 8, TOK), F32),
            pltpu.VMEM((NE, NZ, 64, WID), BF16),
            pltpu.VMEM((NE, 32, WID), BF16),
            pltpu.VMEM((NE, 32, WID), BF16),
            pltpu.VMEM((3, NE, 64, WID), BF16),
            pltpu.VMEM((3, NE, 64, WID), BF16),
            pltpu.VMEM((4, 2, 2, PART, D), BF16),
            pltpu.VMEM((4, 2, 4, PART, D), BF16),
            pltpu.VMEM((4, 2, PART // 2, D), BF16),
            pltpu.VMEM((4, 2, PART, D), BF16),
            pltpu.VMEM((4, PART, D), BF16),
            pltpu.VMEM((3, NE, 64, H), F32),
            pltpu.SemaphoreType.DMA((12,)),
            pltpu.SemaphoreType.DMA((4 * 12 + 4 * 8 + 4 * 9 + 4 * 6,)),
            pltpu.SemaphoreType.DMA,
            pltpu.SemaphoreType.DMA,
            pltpu.SemaphoreType.DMA,
            pltpu.SemaphoreType.DMA,
            pltpu.SemaphoreType.DMA((3,)),
            pltpu.SemaphoreType.DMA((2,)),
        ],
        compiler_params=pltpu.CompilerParams(
            collective_id=0, has_side_effects=True, vmem_limit_bytes=64 * 1024 * 1024
        ),
    )(tokens, cotangent, w_gate, w_up, w_down, routes, gates)
    mixed, igrad, scores, gate, up, down = pl.pallas_call(
        hand_over,
        out_shape=shapes,
        in_specs=[vmem] * 6,
        out_specs=(vmem,) * 6,
    )(mixed, igrad, scores, gate, up, down)
    return mixed, igrad, scores, gate, up, down


def body(tokens, routes, gates, cotangent, w_gate, w_up, w_down):
    mixed, igrad, scores, grad_gate, grad_up, grad_down = step(
        tokens, cotangent, w_gate, w_up, jnp.swapaxes(w_down, 1, 2), routes.T, gates.T
    )
    return (mixed, igrad, scores.T, grad_gate, grad_up, jnp.swapaxes(grad_down, 1, 2))


def solution(mesh):
    rows = P(("dp", "expert"), None)
    features = P("expert", "dp", None)
    last = P("expert", None, "dp")
    return jax.shard_map(
        body,
        mesh=mesh,
        in_specs=(rows, rows, rows, rows, features, features, last),
        out_specs=(rows, rows, rows, features, features, last),
        check_vma=False,
    )
```

```python
import jax
import jax.numpy as jnp
from jax import lax
from jax.experimental import pallas as pl
from jax.experimental.pallas import tpu as pltpu
from jax.sharding import PartitionSpec as P

BF16 = jnp.bfloat16
F32 = jnp.float32
D, H, TOK, CAP = 1024, 384, 128, 24
NZ, NY, NX = 8, 4, 4
NE = 4
NP = 8
PAIR_ROWS = 2 * CAP
ROWS = 16 * CAP
WID = 3 * H
PART = TOK // 2
MESH = pl.DeviceIdType.MESH
OFFSETS = (0, -1, 1, 2)
PARTS = (4, 2, 2, 2)
LATER = {2: (1,), 4: (1, 3, 2)}

(
    OWN,
    FORTH,
    BACK,
    FAR,
    PLUS,
    MINUS,
    W_OWN,
    W_UP,
    W_DOWN,
    W_FAR,
    META,
    SELECT_X,
    SELECT_C,
    FWD,
    BWD_A,
    BWD_B,
    PAIR_A,
    PAIR_B,
    RING_UP,
    RING_DOWN,
    RING_END,
    SUM_UP,
    SUM_DOWN,
    SUM_OWN,
    LAST_UP,
    LAST_DOWN,
    LAST,
    MIX,
    IGRAD,
    TURN,
) = range(30)
TA, TB, CA, CB = range(4)

ORDER = (
    (W_OWN, 2), (OWN, CA), (OWN, TA), (W_OWN, 0), (W_OWN, 3), (OWN, TB), (W_UP, 0, 1),
    (MINUS, TA, 0), (BACK, CA), (OWN, CB), (W_DOWN, 0, 1), (W_DOWN, 2, 1), (BACK, TB),
    (MINUS, TB, 0), (W_DOWN, 3, 1), (BACK, TA), (FORTH, TB), (FORTH, TA), (W_UP, 2, 1), (W_OWN, 1),
    (W_UP, 0, 2), (FORTH, CB), (BACK, CB), (PLUS, TB, 2), (FAR, TA), (W_DOWN, 2, 2), (W_UP, 2, 2),
    (PLUS, TA, 2), (PLUS, TB, 1), (FAR, TB), (W_DOWN, 0, 2), (W_UP, 1, 1), (PLUS, TA, 0), (META,),
    (MINUS, TA, 1), (FORTH, CA), (W_UP, 3, 1), (W_UP, 0, 3), (PLUS, CB, 1), (MINUS, TB, 1),
    (W_DOWN, 1, 1), (PLUS, TA, 3), (PLUS, TA, 1), (MINUS, TA, 3), (W_DOWN, 2, 3), (W_DOWN, 0, 3),
    (MINUS, TA, 2), (W_DOWN, 3, 2), (W_UP, 2, 3), (MINUS, TB, 2), (PLUS, TB, 3), (MINUS, TB, 3),
    (FAR, CA), (PLUS, TB, 0), (MINUS, CA, 1), (FAR, CB), (MINUS, CB, 1), (PLUS, CB, 0),
    (MINUS, CB, 2), (PLUS, CA, 0), (W_UP, 1, 2), (PLUS, CB, 2), (W_DOWN, 1, 2), (MINUS, CA, 2),
    (W_FAR, 0), (W_UP, 3, 2), (MINUS, CB, 0), (PLUS, CA, 1), (W_FAR, 2), (SELECT_X,),
    (MINUS, CA, 0), (PLUS, CA, 3), (PLUS, CA, 2), (MINUS, CB, 3), (TURN,), (W_UP, 1, 3),
    (W_DOWN, 3, 3), (MINUS, CA, 3), (PLUS, CB, 3), (FWD, 2), (FWD, 0), (W_DOWN, 1, 3),
    (W_UP, 3, 3), (SELECT_C,), (BWD_A, 0), (W_FAR, 1), (W_FAR, 3), (BWD_B, 0), (PAIR_A, 0),
    (FWD, 1), (FWD, 3), (PAIR_B, 0), (RING_UP, 0, 1), (RING_DOWN, 0, 1), (MIX,), (BWD_A, 2),
    (BWD_A, 3), (RING_DOWN, 0, 2), (RING_UP, 0, 2), (BWD_A, 1), (BWD_B, 1), (PAIR_A, 2),
    (BWD_B, 2), (SUM_DOWN, TB), (PAIR_A, 3), (SUM_UP, TA), (BWD_B, 3), (SUM_UP, TB),
    (RING_DOWN, 0, 3), (SUM_DOWN, TA), (RING_UP, 0, 3), (PAIR_A, 1), (PAIR_B, 3), (PAIR_B, 1),
    (RING_UP, 3, 1), (IGRAD,), (RING_DOWN, 3, 1), (PAIR_B, 2), (RING_END, 0), (RING_DOWN, 2, 1),
    (RING_UP, 2, 1), (RING_DOWN, 3, 2), (RING_UP, 1, 1), (RING_UP, 3, 2), (RING_DOWN, 1, 1),
    (SUM_DOWN, CB), (SUM_DOWN, CA), (SUM_UP, CB), (RING_UP, 1, 2), (RING_UP, 2, 2),
    (RING_DOWN, 2, 2), (SUM_UP, CA), (RING_DOWN, 1, 2), (SUM_OWN, TB), (SUM_OWN, TA),
    (RING_UP, 3, 3), (RING_DOWN, 3, 3), (SUM_OWN, CA), (SUM_OWN, CB), (RING_UP, 2, 3),
    (RING_DOWN, 2, 3), (LAST_DOWN, TB), (LAST_DOWN, TA), (LAST_UP, TA), (LAST_UP, TB),
    (RING_UP, 1, 3), (RING_DOWN, 1, 3), (RING_END, 3), (LAST_UP, CB), (LAST_DOWN, CA),
    (LAST_UP, CA), (LAST_DOWN, CB), (RING_END, 2), (LAST, TA), (LAST, TB), (LAST, CA), (LAST, CB),
    (RING_END, 1),
)


def dot_nt(a, b):
    return lax.dot_general(a, b, (((1,), (1,)), ((), ())), preferred_element_type=F32)


def dot_tn(a, b):
    return lax.dot_general(a, b, (((0,), (0,)), ((), ())), preferred_element_type=F32)


def dot_nn(a, b):
    return lax.dot_general(a, b, (((1,), (0,)), ((), ())), preferred_element_type=F32)


def kernel(
    tok_ref, cot_ref, wg_ref, wu_ref, wd_ref, routes_ref, gates_ref,
    mixed_ref, igrad_ref, gg_ref, out_gate, out_up, out_down,
    xbuf, cbuf, wbuf, mbuf, slot, gate, onehot, weighted, hot_t, weighted_t, xe, se, lin, hid, both_ref, orow, rrow, gsend, grecv,
    pr, ru1, rd1, ru, rd, a1, a2, b1, b2, fout, gout,
    send_sems, recv_sems, msend, mrecv, gsem_s, gsem_r, local_sems, out_sems,
):
    dp, ex = lax.axis_index("dp"), lax.axis_index("expert")
    z, c = lax.div(dp, 2), lax.rem(dp, 2)
    y, x = lax.div(ex, NX), lax.rem(ex, NX)
    sibling = (2 * z + (1 - c), ex)

    def mod(a, n):
        return lax.rem(a + n, n)

    def zdev(o):
        return (2 * mod(z + o, NZ) + c, ex)

    def zpos(o):
        return 2 * mod(z + o, NZ) + c

    def plane(oy, ox):
        return mod(y + oy, NY) * NX + mod(x + ox, NX)

    def plane_dev(oy, ox):
        return (dp, plane(oy, ox))

    barrier = pltpu.get_barrier_semaphore()

    def greet(i, _):
        pl.semaphore_signal(barrier, inc=1, device_id=(dp, lax.rem(ex + i, 16)), device_id_type=MESH)
        return 0

    lax.fori_loop(1, 16, greet, 0)
    for dev in (sibling, zdev(1), zdev(-1)):
        pl.semaphore_signal(barrier, inc=1, device_id=dev, device_id_type=MESH)
    local = [
        pltpu.make_async_copy(tok_ref, xbuf.at[ex], local_sems.at[0]),
        pltpu.make_async_copy(cot_ref, cbuf.at[ex], local_sems.at[1]),
        pltpu.make_async_copy(wg_ref, wbuf.at[:, dp, :, pl.ds(0, H)], local_sems.at[2]),
        pltpu.make_async_copy(wu_ref, wbuf.at[:, dp, :, pl.ds(H, H)], local_sems.at[2]),
        pltpu.make_async_copy(wd_ref, wbuf.at[:, dp, :, pl.ds(2 * H, H)], local_sems.at[2]),
    ]
    for copy in local:
        copy.start()
    mbuf[ex, 0:8, :] = routes_ref[...].astype(F32)
    mbuf[ex, 8:16, :] = gates_ref[...]
    gsend[...] = jnp.zeros_like(gsend)
    pl.semaphore_wait(barrier, 18)

    arrivals, departures, pending, actions = {}, {}, {}, {}

    def send(key, src, dst, dev, group):
        copy = pltpu.make_async_remote_copy(
            src_ref=src,
            dst_ref=dst,
            send_sem=send_sems.at[departures.setdefault(group, len(departures))],
            recv_sem=recv_sems.at[arrivals.setdefault(key, len(arrivals))],
            device_id=dev,
            device_id_type=MESH,
        )
        copy.start()
        pending[key] = copy

    def wait(*key):
        pending.pop(key).wait_recv()

    def wait_all(ref, *key):
        pltpu.make_async_copy(ref, ref, recv_sems.at[arrivals[key]]).wait()

    def drain(ref, group):
        pltpu.make_async_copy(ref, ref, send_sems.at[departures[group]]).wait()

    def plane_axes(first):
        if first == "y":
            return (lambda o: plane_dev(o, 0)), (lambda o: plane_dev(0, o)), plane
        return (lambda o: plane_dev(0, o)), (lambda o: plane_dev(o, 0)), (lambda a, b: plane(b, a))

    def gather(n, group, arg, buf, first, lo):
        dev1, dev2, pos = plane_axes(first)
        halves = (pl.ds(lo, PART // 2), pl.ds(lo + PART // 2, PART // 2))

        def move(key, a, b, dev, rows):
            ref = buf.at[pos(a, b), rows]
            send((n,) + key, arg.at[rows] if (a, b) == (0, 0) else ref, ref, dev, group)

        whole = pl.ds(lo, PART)

        def second(i):
            move(("p", i), OFFSETS[i], 0, dev2(1), whole)
            move(("m", i), OFFSETS[i], 0, dev2(-1), whole)

        def own():
            move(("r1p",), 0, 0, dev1(1), whole)
            move(("r1m",), 0, 0, dev1(-1), whole)
            second(0)

        def forward():
            wait(n, "r1p")
            move(("r2",), -1, 0, dev1(1), halves[0])
            second(1)

        def backward():
            wait(n, "r1m")
            move(("r2",), 1, 0, dev1(-1), halves[1])
            second(2)

        def opposite():
            wait_all(buf.at[0, whole], n, "r2")
            second(3)

        def plus(i):
            wait(n, "p", i)
            move(("last",), OFFSETS[i], -1, dev2(1), halves[0])

        def minus(i):
            wait(n, "m", i)
            move(("last",), OFFSETS[i], 1, dev2(-1), halves[1])

        actions[OWN, n] = own
        actions[FORTH, n] = forward
        actions[BACK, n] = backward
        actions[FAR, n] = opposite
        for i in range(4):
            actions[PLUS, n, i] = lambda i=i: plus(i)
            actions[MINUS, n, i] = lambda i=i: minus(i)

    gather(TA, "t", tok_ref, xbuf, "x", 0)
    gather(TB, "t", tok_ref, xbuf, "y", PART)
    gather(CA, "c", cot_ref, cbuf, "x", 0)
    gather(CB, "c", cot_ref, cbuf, "y", PART)

    def gathered(arrays, copy, buf):
        copy.wait()
        for n in arrays:
            wait_all(buf.at[pl.ds(0, 4), pl.ds(0, PART)], n, "last")

    own_weights = [wbuf.at[:, dp]]

    def weight(e):
        def move(key, o, dev, rows=None):
            ref = wbuf.at[e, zpos(o)]
            if rows is not None:
                ref = ref.at[rows]
            send(("w", e) + key, ref, ref, dev, ("w", e))

        def own():
            if own_weights:
                pltpu.make_async_copy(own_weights[0], own_weights.pop(), local_sems.at[2]).wait()
            move(("u", 1), 0, zdev(1))
            move(("d", 1), 0, zdev(-1))
            move(("s",), 0, sibling)

        def up(k):
            wait("w", e, "u", k)
            move(("far",) if k == 3 else ("u", k + 1), -k, zdev(1), pl.ds(0, 32) if k == 3 else None)
            move(("s",), -k, sibling)

        def down(k):
            wait("w", e, "d", k)
            move(("far",) if k == 3 else ("d", k + 1), k, zdev(-1), pl.ds(32, 32) if k == 3 else None)
            move(("s",), k, sibling)

        def opposite():
            wait_all(wbuf.at[e, 0], "w", e, "far")
            move(("s",), 4, sibling)

        actions[W_OWN, e] = own
        actions[W_FAR, e] = opposite
        for k in (1, 2, 3):
            actions[W_UP, e, k] = lambda k=k: up(k)
            actions[W_DOWN, e, k] = lambda k=k: down(k)

    for e in range(NE):
        weight(e)

    def meta_copy(i):
        return pltpu.make_async_remote_copy(
            src_ref=mbuf.at[ex],
            dst_ref=mbuf.at[ex],
            send_sem=msend,
            recv_sem=mrecv,
            device_id=(dp, lax.rem(ex + i, 16)),
            device_id_type=MESH,
        )

    def meta_start(i, _):
        meta_copy(i).start()
        return 0

    def meta():
        for sem in (msend, mrecv):
            pltpu.make_async_copy(mbuf.at[pl.ds(0, 15)], mbuf.at[pl.ds(0, 15)], sem).wait()
        lower = (
            lax.broadcasted_iota(jnp.int32, (TOK, TOK), 0)
            < lax.broadcasted_iota(jnp.int32, (TOK, TOK), 1)
        ).astype(F32).astype(BF16)
        paired = mbuf.reshape(NP, 2, 16, TOK)
        for odd in range(2):
            names = paired[:, odd, 0:8, :]
            values = paired[:, odd, 8:16, :]
            cols = slice(odd * TOK, (odd + 1) * TOK)
            for j in range(NE):
                hit = names == (NE * ex + j).astype(F32)
                member = jnp.max(jnp.where(hit, 1.0, 0.0), axis=1)
                rank = dot_nn(member.astype(BF16), lower)
                slot[j, :, cols] = jnp.where(member > 0.5, rank + float(odd * CAP), -1000.0)
                gate[j, :, cols] = jnp.sum(jnp.where(hit, values, 0.0), axis=1)
        places = lax.broadcasted_iota(jnp.int32, (PAIR_ROWS, 2 * TOK), 0).astype(F32)

        def build(p, _):
            for j in range(NE):
                part = slice(j * PAIR_ROWS, (j + 1) * PAIR_ROWS)
                hit = slot[j, pl.ds(p, 1), :] == places
                onehot[p, part, :] = jnp.where(hit, 1.0, 0.0).astype(BF16)
                weighted[p, part, :] = jnp.where(hit, gate[j, pl.ds(p, 1), :], 0.0).astype(BF16)
            return 0

        lax.fori_loop(0, NP, build, 0)

    actions[(META,)] = meta

    def turn():
        def body(p, _):
            hot_t[p] = onehot[p].T
            weighted_t[p] = weighted[p].T
            return 0

        lax.fori_loop(0, NP, body, 0)

    actions[(TURN,)] = turn

    def pair_at(p):
        return pl.ds(pl.multiple_of(p * PAIR_ROWS, 16), PAIR_ROWS)

    def select_tokens():
        gathered((TA, TB), local[0], xbuf)

        def body(p, _):
            rows = dot_nn(onehot[p], xbuf[pl.ds(2 * p, 2)].reshape(2 * TOK, D)).astype(BF16)
            for j in range(NE):
                xe[j, pair_at(p), :] = rows[j * PAIR_ROWS : (j + 1) * PAIR_ROWS]
            return 0

        lax.fori_loop(0, NP, body, 0, unroll=4)

    def select_cotangent():
        gathered((CA, CB), local[1], cbuf)

        def body(p, _):
            rows = dot_nn(weighted[p], cbuf[pl.ds(2 * p, 2)].reshape(2 * TOK, D)).astype(BF16)
            for j in range(NE):
                se[j, pair_at(p), :] = rows[j * PAIR_ROWS : (j + 1) * PAIR_ROWS]
            return 0

        lax.fori_loop(0, NP, body, 0, unroll=4)

    actions[(SELECT_X,)] = select_tokens
    actions[(SELECT_C,)] = select_cotangent

    def forward(e):
        wait_all(wbuf.at[e, pl.ds(0, 8)], "w", e, "s")
        gate_up = dot_nn(xe[e], wbuf[e, :, :, 0 : 2 * H].reshape(D, 2 * H))
        lin[e] = gate_up
        linear, up = gate_up[:, :H], gate_up[:, H:]
        sig = 1.0 / (1.0 + jnp.exp(-linear))
        hidden = (linear * sig * up).astype(BF16)
        hid[e] = hidden
        out = dot_nt(hidden, wbuf[e, :, :, 2 * H : WID].reshape(D, H))
        orow[:, e * PAIR_ROWS : (e + 1) * PAIR_ROWS, :] = out.astype(BF16).reshape(NP, PAIR_ROWS, D)

    grads = wbuf.reshape(NE, NZ, 2, 64, WID)
    def place(e, o):
        parts = PARTS[e]
        span = NZ // parts
        return lax.rem(lax.div(z, span) + parts // 2 + o, parts)

    def part_grads(e, o):
        q, n, m = place(e, o), 16 // PARTS[e], D // PARTS[e]
        blocks, cols = pl.ds(n * q, n), pl.ds(pl.multiple_of(m * q, m), m)
        both, hidden = both_ref[e], hid[e]
        back = dot_nt(both, wbuf[e, blocks, :, 0 : 2 * H].reshape(m, 2 * H))
        rrow[:, e * PAIR_ROWS : (e + 1) * PAIR_ROWS, cols] = (
            back.astype(BF16).reshape(NP, PAIR_ROWS, m)
        )
        wbuf[e, blocks, :, 0 : 2 * H] = (
            dot_tn(xe[e, :, cols], both).astype(BF16).reshape(n, 64, 2 * H)
        )
        wbuf[e, blocks, :, 2 * H : WID] = (
            dot_tn(se[e, :, cols], hidden).astype(BF16).reshape(n, 64, H)
        )

    def pair_send(e, o):
        span = NZ // PARTS[e]
        at = pl.ds(span * place(e, o), span)
        send(("pair", e, o > 0), grads.at[e, at, 1 - c], pr.at[e, at], sibling, ("z", e))

    def backward_first(e):
        drain(wbuf.at[e, pl.ds(0, 15)], ("w", e))
        hidden_grad = dot_nn(se[e], wbuf[e, :, :, 2 * H : WID].reshape(D, H))
        linear, up = lin[e, :, :H], lin[e, :, H:]
        sig = 1.0 / (1.0 + jnp.exp(-linear))
        up_grad = (hidden_grad * linear * sig).astype(BF16)
        gate_grad = (hidden_grad * up * sig * (1.0 + linear * (1.0 - sig))).astype(BF16)
        products = jnp.sum(hid[e].astype(F32) * hidden_grad, axis=1, keepdims=True)
        for p in range(NP):
            hot = onehot[p, e * PAIR_ROWS : (e + 1) * PAIR_ROWS, :].astype(F32)
            sums = jnp.sum(hot * products[p * PAIR_ROWS : (p + 1) * PAIR_ROWS], axis=0, keepdims=True)
            scale = gate[e, p : p + 1, :].astype(BF16).astype(F32)
            sums = jnp.where(scale > 0.0, sums / jnp.where(scale > 0.0, scale, 1.0), 0.0)
            for odd in range(2):
                gsend[2 * p + odd, e : e + 1, :] = sums[:, odd * TOK : (odd + 1) * TOK]
        both_ref[e, :, :H] = gate_grad
        both_ref[e, :, H:] = up_grad
        part_grads(e, 0)
        pair_send(e, 0)

    def backward_rest(e):
        for o in LATER[PARTS[e]]:
            part_grads(e, o)
            pair_send(e, o)

    def add_pair(e, parts):
        span = NZ // PARTS[e]
        wait_all(pr.at[e, pl.ds(0, span * len(parts))], "pair", e, parts[0] > 0)
        for o in parts:
            for i in range(span):
                at = span * place(e, o) + i
                pr[e, at] = (pr[e, at].astype(F32) + grads[e, at, c].astype(F32)).astype(BF16)

    def ring_start(e):
        add_pair(e, (0,))
        opposite = mod(z + 4, NZ)
        send(("ru", e, 1), pr.at[e, opposite, pl.ds(0, 32)], ru1.at[e], zdev(1), ("z", e))
        send(("rd", e, 1), pr.at[e, opposite, pl.ds(32, 32)], rd1.at[e], zdev(-1), ("z", e))

    def ring_rest(e):
        add_pair(e, LATER[PARTS[e]])

    def ring(e, k, sign):
        name, one, many = ("ru", ru1, ru) if sign == 1 else ("rd", rd1, rd)
        at = mod(z + sign * (4 - k), NZ)
        wait(name, e, k)
        if k == 1:
            rows = pl.ds(0, 32) if sign == 1 else pl.ds(32, 32)
            pr[e, at, rows] = (pr[e, at, rows].astype(F32) + one[e].astype(F32)).astype(BF16)
        else:
            pr[e, at] = (pr[e, at].astype(F32) + many[k - 2, e].astype(F32)).astype(BF16)
        key = ("end", e) if k == 3 else (name, e, k + 1)
        send(key, pr.at[e, at], many.at[k - 1, e], zdev(sign), ("z", e))

    def put(src, dst, k):
        pltpu.make_async_copy(src, dst, out_sems.at[k]).start()

    def ring_end(e):
        wait_all(pr.at[e, pl.ds(0, 2)], "end", e)
        total = pr[e, z].astype(F32) + ru[2, e].astype(F32) + rd[2, e].astype(F32)
        for i, ref in enumerate((out_gate, out_up, out_down)):
            gout[i, e] = total[:, i * H : (i + 1) * H]
            put(gout.at[i, e], ref.at[e], 1)

    for e in range(NE):
        actions[FWD, e] = lambda e=e: forward(e)
        actions[BWD_A, e] = lambda e=e: backward_first(e)
        actions[BWD_B, e] = lambda e=e: backward_rest(e)
        actions[PAIR_A, e] = lambda e=e: ring_start(e)
        actions[PAIR_B, e] = lambda e=e: ring_rest(e)
        actions[RING_END, e] = lambda e=e: ring_end(e)
        for k in (1, 2, 3):
            actions[RING_UP, e, k] = lambda e=e, k=k: ring(e, k, 1)
            actions[RING_DOWN, e, k] = lambda e=e, k=k: ring(e, k, -1)

    def scatter(n, buf, out, first, lo, group_of_sends):
        dev1, dev2, _ = plane_axes(first)
        blocks = buf.reshape(NY, NX, TOK, D)
        whole = pl.ds(lo, PART)
        halves = (pl.ds(lo, PART // 2), pl.ds(lo + PART // 2, PART // 2))
        local_halves = (pl.ds(0, PART // 2), pl.ds(PART // 2, PART // 2))
        mine, other = (y, x) if first == "y" else (x, y)

        def group(o, at, count):
            if first == "y":
                return blocks.at[mod(mine + o, 4), pl.ds(at, count), whole]
            return blocks.at[pl.ds(at, count), mod(mine + o, 4), whole]

        def own(o, rows):
            if first == "y":
                return blocks.at[mine, mod(other + o, 4), rows]
            return blocks.at[mod(other + o, 4), mine, rows]

        def start():
            yield lambda: send((n, "a1p"), group(2, 0, 2), a1.at[n, 0], dev1(1), group_of_sends)
            yield lambda: send((n, "a1m"), group(2, 2, 2), a1.at[n, 1], dev1(-1), group_of_sends)
            yield lambda: send(
                (n, "a2"), group(1, 2, 2), a2.at[n, 0, pl.ds(2, 2)], dev1(1), group_of_sends
            )
            yield lambda: send(
                (n, "a2"), group(-1, 0, 2), a2.at[n, 1, pl.ds(0, 2)], dev1(-1), group_of_sends
            )

        def add(key, k, o, at, name):
            wait(n, key)
            ref = group(o, at, 2)
            for i in range(2):
                ref[i] = (ref[i].astype(F32) + a1[n, k, i].astype(F32)).astype(BF16)
            send((n, name), ref, a2.at[n, k, pl.ds(at, 2)], dev1(o), group_of_sends)

        def total():
            wait_all(a2.at[n], n, "a2")
            for o in (2, 1, -1, 0):
                ref, at = own(o, whole), mod(other + o, 4)
                ref[...] = (
                    ref[...].astype(F32)
                    + a2[n, 0, at].astype(F32)
                    + a2[n, 1, at].astype(F32)
                ).astype(BF16)
                if o == 2:
                    send((n, "b1p"), own(2, halves[0]), b1.at[n, 0], dev2(1), group_of_sends)
                    send((n, "b1m"), own(2, halves[1]), b1.at[n, 1], dev2(-1), group_of_sends)
                if o == 1:
                    send(
                        (n, "b2"), own(1, halves[1]), b2.at[n, 0, local_halves[1]], dev2(1), group_of_sends
                    )
                if o == -1:
                    send(
                        (n, "b2"), own(-1, halves[0]), b2.at[n, 1, local_halves[0]], dev2(-1), group_of_sends
                    )

        def add_second(key, k, o, name):
            wait(n, key)
            ref = own(o, halves[k])
            ref[...] = (ref[...].astype(F32) + b1[n, k].astype(F32)).astype(BF16)
            send((n, name), ref, b2.at[n, k, local_halves[k]], dev2(o), group_of_sends)

        def finish():
            wait_all(b2.at[n], n, "b2")
            fout[n] = (
                own(0, whole)[...].astype(F32)
                + b2[n, 0].astype(F32)
                + b2[n, 1].astype(F32)
            ).astype(BF16)
            put(fout.at[n], out.at[whole], 0)

        actions[SUM_UP, n] = lambda: add("a1p", 0, 1, 0, "a2")
        actions[SUM_DOWN, n] = lambda: add("a1m", 1, -1, 2, "a2")
        actions[SUM_OWN, n] = total
        actions[LAST_UP, n] = lambda: add_second("b1p", 0, 1, "b2")
        actions[LAST_DOWN, n] = lambda: add_second("b1m", 1, -1, "b2")
        actions[LAST, n] = finish
        return start

    starts = {
        "m": (
            scatter(TA, xbuf, mixed_ref, "y", 0, "m"),
            scatter(TB, xbuf, mixed_ref, "x", PART, "m"),
        ),
        "i": (
            scatter(CA, cbuf, igrad_ref, "x", 0, "i"),
            scatter(CB, cbuf, igrad_ref, "y", PART, "i"),
        ),
    }

    def start_sums(n):
        for one, two in zip(starts[n][0](), starts[n][1]()):
            one()
            two()

    def mix():
        drain(xbuf.at[pl.ds(0, 15)], "t")

        def body(p, _):
            mixed = dot_nn(weighted_t[p], orow[p])
            xbuf[pl.ds(2 * p, 2)] = mixed.astype(BF16).reshape(2, TOK, D)
            return 0

        lax.fori_loop(0, NP, body, 0, unroll=4)
        start_sums("m")

    def gg_copy(i):
        return pltpu.make_async_remote_copy(
            src_ref=gsend.at[lax.rem(ex + i, 16)],
            dst_ref=grecv.at[ex],
            send_sem=gsem_s,
            recv_sem=gsem_r,
            device_id=(dp, lax.rem(ex + i, 16)),
            device_id_type=MESH,
        )

    def gg_start(i, _):
        gg_copy(i).start()
        return 0

    def input_grads():
        drain(cbuf.at[pl.ds(0, 15)], "c")

        def body(p, _):
            back = dot_nn(hot_t[p], rrow[p])
            cbuf[pl.ds(2 * p, 2)] = back.astype(BF16).reshape(2, TOK, D)
            return 0

        lax.fori_loop(0, NP, body, 0, unroll=4)
        start_sums("i")
        lax.fori_loop(1, 16, gg_start, 0)

    actions[(MIX,)] = mix
    actions[(IGRAD,)] = input_grads

    lax.fori_loop(1, 16, meta_start, 0)
    for name in ORDER:
        actions[name]()

    for sem in (gsem_s, gsem_r):
        pltpu.make_async_copy(grecv.at[pl.ds(0, 15)], grecv.at[pl.ds(0, 15)], sem).wait()
    grecv[ex] = gsend[ex]
    named = routes_ref[...]
    total = jnp.zeros((8, TOK), F32)
    for owner in range(16):
        for j in range(NE):
            total = total + jnp.where(named == NE * owner + j, grecv[owner, j : j + 1, :], 0.0)
    gg_ref[...] = total
    drain(xbuf.at[pl.ds(0, 15)], "m")
    drain(cbuf.at[pl.ds(0, 15)], "i")
    for e in range(NE):
        drain(wbuf.at[e, pl.ds(0, 15)], ("z", e))
    pltpu.make_async_copy(fout, fout, out_sems.at[0]).wait()
    pltpu.make_async_copy(gout, gout, out_sems.at[1]).wait()


def hand_over(*refs):
    for src, dst in zip(refs[:6], refs[6:]):
        dst[...] = src[...]


def step(tokens, cotangent, w_gate, w_up, w_down, routes, gates):
    any_spec = pl.BlockSpec(memory_space=pl.ANY)
    vmem = pl.BlockSpec(memory_space=pltpu.VMEM)
    out = jax.ShapeDtypeStruct
    shapes = (
        out((TOK, D), BF16),
        out((TOK, D), BF16),
        out((8, TOK), F32),
        out((NE, 64, H), F32),
        out((NE, 64, H), F32),
        out((NE, 64, H), F32),
    )
    mixed, igrad, scores, gate, up, down = pl.pallas_call(
        kernel,
        out_shape=shapes,
        in_specs=[any_spec] * 5 + [vmem] * 2,
        out_specs=(any_spec, any_spec, vmem, any_spec, any_spec, any_spec),
        scratch_shapes=[
            pltpu.VMEM((16, TOK, D), BF16),
            pltpu.VMEM((16, TOK, D), BF16),
            pltpu.VMEM((NE, 16, 64, WID), BF16),
            pltpu.VMEM((16, 16, TOK), F32),
            pltpu.VMEM((NE, NP, 2 * TOK), F32),
            pltpu.VMEM((NE, NP, 2 * TOK), F32),
            pltpu.VMEM((NP, NE * PAIR_ROWS, 2 * TOK), BF16),
            pltpu.VMEM((NP, NE * PAIR_ROWS, 2 * TOK), BF16),
            pltpu.VMEM((NP, 2 * TOK, NE * PAIR_ROWS), BF16),
            pltpu.VMEM((NP, 2 * TOK, NE * PAIR_ROWS), BF16),
            pltpu.VMEM((NE, ROWS, D), BF16),
            pltpu.VMEM((NE, ROWS, D), BF16),
            pltpu.VMEM((NE, ROWS, 2 * H), F32),
            pltpu.VMEM((NE, ROWS, H), BF16),
            pltpu.VMEM((NE, ROWS, 2 * H), BF16),
            pltpu.VMEM((NP, NE * PAIR_ROWS, D), BF16),
            pltpu.VMEM((NP, NE * PAIR_ROWS, D), BF16),
            pltpu.VMEM((16, 8, TOK), F32),
            pltpu.VMEM((16, 8, TOK), F32),
            pltpu.VMEM((NE, NZ, 64, WID), BF16),
            pltpu.VMEM((NE, 32, WID), BF16),
            pltpu.VMEM((NE, 32, WID), BF16),
            pltpu.VMEM((3, NE, 64, WID), BF16),
            pltpu.VMEM((3, NE, 64, WID), BF16),
            pltpu.VMEM((4, 2, 2, PART, D), BF16),
            pltpu.VMEM((4, 2, 4, PART, D), BF16),
            pltpu.VMEM((4, 2, PART // 2, D), BF16),
            pltpu.VMEM((4, 2, PART, D), BF16),
            pltpu.VMEM((4, PART, D), BF16),
            pltpu.VMEM((3, NE, 64, H), F32),
            pltpu.SemaphoreType.DMA((12,)),
            pltpu.SemaphoreType.DMA((4 * 12 + 4 * 8 + 4 * 9 + 4 * 6,)),
            pltpu.SemaphoreType.DMA,
            pltpu.SemaphoreType.DMA,
            pltpu.SemaphoreType.DMA,
            pltpu.SemaphoreType.DMA,
            pltpu.SemaphoreType.DMA((3,)),
            pltpu.SemaphoreType.DMA((2,)),
        ],
        compiler_params=pltpu.CompilerParams(
            collective_id=0, has_side_effects=True, vmem_limit_bytes=64 * 1024 * 1024
        ),
    )(tokens, cotangent, w_gate, w_up, w_down, routes, gates)
    rows = pl.BlockSpec((TOK // 2, D), lambda i: (i, 0))
    experts = pl.BlockSpec((NE // 2, 64, H), lambda i: (i, 0, 0))
    blocks = (rows, rows, pl.BlockSpec((8, TOK), lambda i: (0, 0)), experts, experts, experts)
    mixed, igrad, scores, gate, up, down = pl.pallas_call(
        hand_over,
        grid=(2,),
        out_shape=shapes,
        in_specs=blocks,
        out_specs=blocks,
    )(mixed, igrad, scores, gate, up, down)
    return mixed, igrad, scores, gate, up, down


def body(tokens, routes, gates, cotangent, w_gate, w_up, w_down):
    mixed, igrad, scores, grad_gate, grad_up, grad_down = step(
        tokens, cotangent, w_gate, w_up, jnp.swapaxes(w_down, 1, 2), routes.T, gates.T
    )
    return (mixed, igrad, scores.T, grad_gate, grad_up, jnp.swapaxes(grad_down, 1, 2))


def solution(mesh):
    rows = P(("dp", "expert"), None)
    features = P("expert", "dp", None)
    last = P("expert", None, "dp")
    return jax.shard_map(
        body,
        mesh=mesh,
        in_specs=(rows, rows, rows, rows, features, features, last),
        out_specs=(rows, rows, rows, features, features, last),
        check_vma=False,
    )
```

```python
import jax
import jax.numpy as jnp
from jax import lax
from jax.experimental import pallas as pl
from jax.experimental.pallas import tpu as pltpu
from jax.sharding import PartitionSpec as P

BF16 = jnp.bfloat16
F32 = jnp.float32
D, H, TOK, CAP = 1024, 384, 128, 24
NZ, NY, NX = 8, 4, 4
NE = 4
NP = 8
PAIR_ROWS = 2 * CAP
ROWS = 16 * CAP
WID = 3 * H
PART = TOK // 2
MESH = pl.DeviceIdType.MESH
OFFSETS = (0, -1, 1, 2)
PARTS = (4, 2, 2, 2)
LATER = {2: (1,), 4: (1, 3, 2)}

(
    OWN,
    FORTH,
    BACK,
    FAR,
    PLUS,
    MINUS,
    W_OWN,
    W_UP,
    W_DOWN,
    W_FAR,
    META,
    SELECT_X,
    SELECT_C,
    FWD,
    BWD_A,
    BWD_B,
    PAIR_A,
    PAIR_B,
    RING_UP,
    RING_DOWN,
    RING_END,
    SUM_UP,
    SUM_DOWN,
    SUM_OWN,
    LAST_UP,
    LAST_DOWN,
    LAST,
    MIX,
    IGRAD,
    TURN,
    MIX_A,
) = range(31)
TA, TB, CA, CB = range(4)

ORDER = (
    (W_OWN, 2), (OWN, CA), (OWN, TA), (W_OWN, 0), (W_OWN, 3), (OWN, TB), (W_UP, 0, 1),
    (MINUS, TA, 0), (BACK, CA), (OWN, CB), (W_DOWN, 0, 1), (W_DOWN, 2, 1), (BACK, TB),
    (MINUS, TB, 0), (W_DOWN, 3, 1), (BACK, TA), (FORTH, TB), (FORTH, TA), (W_UP, 2, 1), (W_OWN, 1),
    (W_UP, 0, 2), (FORTH, CB), (BACK, CB), (PLUS, TB, 2), (FAR, TA), (W_DOWN, 2, 2), (W_UP, 2, 2),
    (PLUS, TA, 2), (PLUS, TB, 1), (FAR, TB), (W_DOWN, 0, 2), (W_UP, 1, 1), (PLUS, TA, 0), (META,),
    (MINUS, TA, 1), (FORTH, CA), (W_UP, 3, 1), (W_UP, 0, 3), (PLUS, CB, 1), (MINUS, TB, 1),
    (W_DOWN, 1, 1), (PLUS, TA, 3), (PLUS, TA, 1), (MINUS, TA, 3), (W_DOWN, 2, 3), (W_DOWN, 0, 3),
    (MINUS, TA, 2), (W_DOWN, 3, 2), (W_UP, 2, 3), (MINUS, TB, 2), (PLUS, TB, 3), (MINUS, TB, 3),
    (FAR, CA), (PLUS, TB, 0), (MINUS, CA, 1), (FAR, CB), (MINUS, CB, 1), (PLUS, CB, 0),
    (MINUS, CB, 2), (PLUS, CA, 0), (W_UP, 1, 2), (PLUS, CB, 2), (W_DOWN, 1, 2), (MINUS, CA, 2),
    (W_FAR, 0), (W_UP, 3, 2), (MINUS, CB, 0), (PLUS, CA, 1), (W_FAR, 2), (SELECT_X,),
    (MINUS, CA, 0), (PLUS, CA, 3), (PLUS, CA, 2), (MINUS, CB, 3), (TURN,), (W_UP, 1, 3),
    (W_DOWN, 3, 3), (MINUS, CA, 3), (PLUS, CB, 3), (FWD, 2), (FWD, 0), (W_DOWN, 1, 3),
    (W_UP, 3, 3), (SELECT_C,), (BWD_A, 0), (W_FAR, 1), (W_FAR, 3), (BWD_B, 0), (PAIR_A, 0),
    (FWD, 1), (FWD, 3), (PAIR_B, 0), (RING_UP, 0, 1), (RING_DOWN, 0, 1), (MIX_A,), (MIX,),
    (BWD_A, 2), (BWD_A, 3), (RING_DOWN, 0, 2), (RING_UP, 0, 2), (BWD_A, 1), (BWD_B, 1),
    (PAIR_A, 2), (BWD_B, 2), (SUM_DOWN, TB), (PAIR_A, 3), (SUM_UP, TA), (BWD_B, 3), (SUM_UP, TB),
    (RING_DOWN, 0, 3), (SUM_DOWN, TA), (RING_UP, 0, 3), (PAIR_A, 1), (PAIR_B, 3), (PAIR_B, 1),
    (RING_UP, 3, 1), (IGRAD,), (RING_DOWN, 3, 1), (PAIR_B, 2), (RING_END, 0), (RING_DOWN, 2, 1),
    (RING_UP, 2, 1), (RING_DOWN, 3, 2), (RING_UP, 1, 1), (RING_UP, 3, 2), (RING_DOWN, 1, 1),
    (SUM_DOWN, CB), (SUM_DOWN, CA), (SUM_UP, CB), (RING_UP, 1, 2), (RING_UP, 2, 2),
    (RING_DOWN, 2, 2), (SUM_UP, CA), (RING_DOWN, 1, 2), (SUM_OWN, TB), (SUM_OWN, TA),
    (RING_UP, 3, 3), (RING_DOWN, 3, 3), (SUM_OWN, CA), (SUM_OWN, CB), (RING_UP, 2, 3),
    (RING_DOWN, 2, 3), (LAST_DOWN, TB), (LAST_DOWN, TA), (LAST_UP, TA), (LAST_UP, TB),
    (RING_UP, 1, 3), (RING_DOWN, 1, 3), (RING_END, 3), (LAST_UP, CB), (LAST_DOWN, CA),
    (LAST_UP, CA), (LAST_DOWN, CB), (RING_END, 2), (LAST, TA), (LAST, TB), (LAST, CA), (LAST, CB),
    (RING_END, 1),
)


def dot_nt(a, b):
    return lax.dot_general(a, b, (((1,), (1,)), ((), ())), preferred_element_type=F32)


def dot_tn(a, b):
    return lax.dot_general(a, b, (((0,), (0,)), ((), ())), preferred_element_type=F32)


def dot_nn(a, b):
    return lax.dot_general(a, b, (((1,), (0,)), ((), ())), preferred_element_type=F32)


def kernel(
    tok_ref, cot_ref, wg_ref, wu_ref, wd_ref, routes_ref, gates_ref,
    mixed_ref, igrad_ref, gg_ref, out_gate, out_up, out_down,
    xbuf, cbuf, wbuf, mbuf, slot, gate, onehot, weighted, hot_t, weighted_t, xe, se, lin, hid, both_ref, orow, rrow, gsend, grecv,
    pr, ru1, rd1, ru, rd, a1, a2, b1, b2, fout, gout,
    send_sems, recv_sems, msend, mrecv, gsem_s, gsem_r, local_sems, out_sems,
):
    dp, ex = lax.axis_index("dp"), lax.axis_index("expert")
    z, c = lax.div(dp, 2), lax.rem(dp, 2)
    y, x = lax.div(ex, NX), lax.rem(ex, NX)
    sibling = (2 * z + (1 - c), ex)

    def mod(a, n):
        return lax.rem(a + n, n)

    def zdev(o):
        return (2 * mod(z + o, NZ) + c, ex)

    def zpos(o):
        return 2 * mod(z + o, NZ) + c

    def plane(oy, ox):
        return mod(y + oy, NY) * NX + mod(x + ox, NX)

    def plane_dev(oy, ox):
        return (dp, plane(oy, ox))

    barrier = pltpu.get_barrier_semaphore()

    def greet(i, _):
        pl.semaphore_signal(barrier, inc=1, device_id=(dp, lax.rem(ex + i, 16)), device_id_type=MESH)
        return 0

    lax.fori_loop(1, 16, greet, 0)
    for dev in (sibling, zdev(1), zdev(-1)):
        pl.semaphore_signal(barrier, inc=1, device_id=dev, device_id_type=MESH)
    local = [
        pltpu.make_async_copy(tok_ref, xbuf.at[ex], local_sems.at[0]),
        pltpu.make_async_copy(cot_ref, cbuf.at[ex], local_sems.at[1]),
        pltpu.make_async_copy(wg_ref, wbuf.at[:, dp, :, pl.ds(0, H)], local_sems.at[2]),
        pltpu.make_async_copy(wu_ref, wbuf.at[:, dp, :, pl.ds(H, H)], local_sems.at[2]),
        pltpu.make_async_copy(wd_ref, wbuf.at[:, dp, :, pl.ds(2 * H, H)], local_sems.at[2]),
    ]
    for copy in local:
        copy.start()
    mbuf[ex, 0:8, :] = routes_ref[...].astype(F32)
    mbuf[ex, 8:16, :] = gates_ref[...]
    gsend[...] = jnp.zeros_like(gsend)
    pl.semaphore_wait(barrier, 18)

    arrivals, departures, pending, actions = {}, {}, {}, {}

    def send(key, src, dst, dev, group):
        copy = pltpu.make_async_remote_copy(
            src_ref=src,
            dst_ref=dst,
            send_sem=send_sems.at[departures.setdefault(group, len(departures))],
            recv_sem=recv_sems.at[arrivals.setdefault(key, len(arrivals))],
            device_id=dev,
            device_id_type=MESH,
        )
        copy.start()
        pending[key] = copy

    def wait(*key):
        pending.pop(key).wait_recv()

    def wait_all(ref, *key):
        pltpu.make_async_copy(ref, ref, recv_sems.at[arrivals[key]]).wait()

    def drain(ref, group):
        pltpu.make_async_copy(ref, ref, send_sems.at[departures[group]]).wait()

    def plane_axes(first):
        if first == "y":
            return (lambda o: plane_dev(o, 0)), (lambda o: plane_dev(0, o)), plane
        return (lambda o: plane_dev(0, o)), (lambda o: plane_dev(o, 0)), (lambda a, b: plane(b, a))

    def gather(n, group, arg, buf, first, lo):
        dev1, dev2, pos = plane_axes(first)
        halves = (pl.ds(lo, PART // 2), pl.ds(lo + PART // 2, PART // 2))

        def move(key, a, b, dev, rows):
            ref = buf.at[pos(a, b), rows]
            send((n,) + key, arg.at[rows] if (a, b) == (0, 0) else ref, ref, dev, group)

        whole = pl.ds(lo, PART)

        def second(i):
            move(("p", i), OFFSETS[i], 0, dev2(1), whole)
            move(("m", i), OFFSETS[i], 0, dev2(-1), whole)

        def own():
            move(("r1p",), 0, 0, dev1(1), whole)
            move(("r1m",), 0, 0, dev1(-1), whole)
            second(0)

        def forward():
            wait(n, "r1p")
            move(("r2",), -1, 0, dev1(1), halves[0])
            second(1)

        def backward():
            wait(n, "r1m")
            move(("r2",), 1, 0, dev1(-1), halves[1])
            second(2)

        def opposite():
            wait_all(buf.at[0, whole], n, "r2")
            second(3)

        def plus(i):
            wait(n, "p", i)
            move(("last",), OFFSETS[i], -1, dev2(1), halves[0])

        def minus(i):
            wait(n, "m", i)
            move(("last",), OFFSETS[i], 1, dev2(-1), halves[1])

        actions[OWN, n] = own
        actions[FORTH, n] = forward
        actions[BACK, n] = backward
        actions[FAR, n] = opposite
        for i in range(4):
            actions[PLUS, n, i] = lambda i=i: plus(i)
            actions[MINUS, n, i] = lambda i=i: minus(i)

    gather(TA, "t", tok_ref, xbuf, "x", 0)
    gather(TB, "t", tok_ref, xbuf, "y", PART)
    gather(CA, "c", cot_ref, cbuf, "x", 0)
    gather(CB, "c", cot_ref, cbuf, "y", PART)

    def gathered(arrays, copy, buf):
        copy.wait()
        for n in arrays:
            wait_all(buf.at[pl.ds(0, 4), pl.ds(0, PART)], n, "last")

    own_weights = [wbuf.at[:, dp]]

    def weight(e):
        def move(key, o, dev, rows=None):
            ref = wbuf.at[e, zpos(o)]
            if rows is not None:
                ref = ref.at[rows]
            send(("w", e) + key, ref, ref, dev, ("w", e))

        def own():
            if own_weights:
                pltpu.make_async_copy(own_weights[0], own_weights.pop(), local_sems.at[2]).wait()
            move(("u", 1), 0, zdev(1))
            move(("d", 1), 0, zdev(-1))
            move(("s",), 0, sibling)

        def up(k):
            wait("w", e, "u", k)
            move(("far",) if k == 3 else ("u", k + 1), -k, zdev(1), pl.ds(0, 32) if k == 3 else None)
            move(("s",), -k, sibling)

        def down(k):
            wait("w", e, "d", k)
            move(("far",) if k == 3 else ("d", k + 1), k, zdev(-1), pl.ds(32, 32) if k == 3 else None)
            move(("s",), k, sibling)

        def opposite():
            wait_all(wbuf.at[e, 0], "w", e, "far")
            move(("s",), 4, sibling)

        actions[W_OWN, e] = own
        actions[W_FAR, e] = opposite
        for k in (1, 2, 3):
            actions[W_UP, e, k] = lambda k=k: up(k)
            actions[W_DOWN, e, k] = lambda k=k: down(k)

    for e in range(NE):
        weight(e)

    def meta_copy(i):
        return pltpu.make_async_remote_copy(
            src_ref=mbuf.at[ex],
            dst_ref=mbuf.at[ex],
            send_sem=msend,
            recv_sem=mrecv,
            device_id=(dp, lax.rem(ex + i, 16)),
            device_id_type=MESH,
        )

    def meta_start(i, _):
        meta_copy(i).start()
        return 0

    def meta():
        for sem in (msend, mrecv):
            pltpu.make_async_copy(mbuf.at[pl.ds(0, 15)], mbuf.at[pl.ds(0, 15)], sem).wait()
        lower = (
            lax.broadcasted_iota(jnp.int32, (TOK, TOK), 0)
            < lax.broadcasted_iota(jnp.int32, (TOK, TOK), 1)
        ).astype(F32).astype(BF16)
        paired = mbuf.reshape(NP, 2, 16, TOK)
        for odd in range(2):
            names = paired[:, odd, 0:8, :]
            values = paired[:, odd, 8:16, :]
            cols = slice(odd * TOK, (odd + 1) * TOK)
            for j in range(NE):
                hit = names == (NE * ex + j).astype(F32)
                member = jnp.max(jnp.where(hit, 1.0, 0.0), axis=1)
                rank = dot_nn(member.astype(BF16), lower)
                slot[j, :, cols] = jnp.where(member > 0.5, rank + float(odd * CAP), -1000.0)
                gate[j, :, cols] = jnp.sum(jnp.where(hit, values, 0.0), axis=1)
        places = lax.broadcasted_iota(jnp.int32, (PAIR_ROWS, 2 * TOK), 0).astype(F32)

        def build(p, _):
            for j in range(NE):
                part = slice(j * PAIR_ROWS, (j + 1) * PAIR_ROWS)
                hit = slot[j, pl.ds(p, 1), :] == places
                onehot[p, part, :] = jnp.where(hit, 1.0, 0.0).astype(BF16)
                weighted[p, part, :] = jnp.where(hit, gate[j, pl.ds(p, 1), :], 0.0).astype(BF16)
            return 0

        lax.fori_loop(0, NP, build, 0)

    actions[(META,)] = meta

    def turn():
        def body(p, _):
            hot_t[p] = onehot[p].T
            weighted_t[p] = weighted[p].T
            return 0

        lax.fori_loop(0, NP, body, 0)

    actions[(TURN,)] = turn

    def pair_at(p):
        return pl.ds(pl.multiple_of(p * PAIR_ROWS, 16), PAIR_ROWS)

    def select_tokens():
        gathered((TA, TB), local[0], xbuf)

        def body(p, _):
            rows = dot_nn(onehot[p], xbuf[pl.ds(2 * p, 2)].reshape(2 * TOK, D)).astype(BF16)
            for j in range(NE):
                xe[j, pair_at(p), :] = rows[j * PAIR_ROWS : (j + 1) * PAIR_ROWS]
            return 0

        lax.fori_loop(0, NP, body, 0, unroll=4)

    def select_cotangent():
        gathered((CA, CB), local[1], cbuf)

        def body(p, _):
            rows = dot_nn(weighted[p], cbuf[pl.ds(2 * p, 2)].reshape(2 * TOK, D)).astype(BF16)
            for j in range(NE):
                se[j, pair_at(p), :] = rows[j * PAIR_ROWS : (j + 1) * PAIR_ROWS]
            return 0

        lax.fori_loop(0, NP, body, 0, unroll=4)

    actions[(SELECT_X,)] = select_tokens
    actions[(SELECT_C,)] = select_cotangent

    def forward(e):
        wait_all(wbuf.at[e, pl.ds(0, 8)], "w", e, "s")
        gate_up = dot_nn(xe[e], wbuf[e, :, :, 0 : 2 * H].reshape(D, 2 * H))
        lin[e] = gate_up
        linear, up = gate_up[:, :H], gate_up[:, H:]
        sig = 1.0 / (1.0 + jnp.exp(-linear))
        hidden = (linear * sig * up).astype(BF16)
        hid[e] = hidden
        out = dot_nt(hidden, wbuf[e, :, :, 2 * H : WID].reshape(D, H))
        orow[:, e * PAIR_ROWS : (e + 1) * PAIR_ROWS, :] = out.astype(BF16).reshape(NP, PAIR_ROWS, D)

    grads = wbuf.reshape(NE, NZ, 2, 64, WID)
    def place(e, o):
        parts = PARTS[e]
        span = NZ // parts
        return lax.rem(lax.div(z, span) + parts // 2 + o, parts)

    def part_grads(e, o):
        q, n, m = place(e, o), 16 // PARTS[e], D // PARTS[e]
        blocks, cols = pl.ds(n * q, n), pl.ds(pl.multiple_of(m * q, m), m)
        both, hidden = both_ref[e], hid[e]
        back = dot_nt(both, wbuf[e, blocks, :, 0 : 2 * H].reshape(m, 2 * H))
        rrow[:, e * PAIR_ROWS : (e + 1) * PAIR_ROWS, cols] = (
            back.astype(BF16).reshape(NP, PAIR_ROWS, m)
        )
        wbuf[e, blocks, :, 0 : 2 * H] = (
            dot_tn(xe[e, :, cols], both).astype(BF16).reshape(n, 64, 2 * H)
        )
        wbuf[e, blocks, :, 2 * H : WID] = (
            dot_tn(se[e, :, cols], hidden).astype(BF16).reshape(n, 64, H)
        )

    def pair_send(e, o):
        span = NZ // PARTS[e]
        at = pl.ds(span * place(e, o), span)
        send(("pair", e, o > 0), grads.at[e, at, 1 - c], pr.at[e, at], sibling, ("z", e))

    def backward_first(e):
        drain(wbuf.at[e, pl.ds(0, 15)], ("w", e))
        hidden_grad = dot_nn(se[e], wbuf[e, :, :, 2 * H : WID].reshape(D, H))
        linear, up = lin[e, :, :H], lin[e, :, H:]
        sig = 1.0 / (1.0 + jnp.exp(-linear))
        up_grad = (hidden_grad * linear * sig).astype(BF16)
        gate_grad = (hidden_grad * up * sig * (1.0 + linear * (1.0 - sig))).astype(BF16)
        products = jnp.sum(hid[e].astype(F32) * hidden_grad, axis=1, keepdims=True)
        for p in range(NP):
            hot = onehot[p, e * PAIR_ROWS : (e + 1) * PAIR_ROWS, :].astype(F32)
            sums = jnp.sum(hot * products[p * PAIR_ROWS : (p + 1) * PAIR_ROWS], axis=0, keepdims=True)
            scale = gate[e, p : p + 1, :].astype(BF16).astype(F32)
            sums = jnp.where(scale > 0.0, sums / jnp.where(scale > 0.0, scale, 1.0), 0.0)
            for odd in range(2):
                gsend[2 * p + odd, e : e + 1, :] = sums[:, odd * TOK : (odd + 1) * TOK]
        both_ref[e, :, :H] = gate_grad
        both_ref[e, :, H:] = up_grad
        part_grads(e, 0)
        pair_send(e, 0)

    def backward_rest(e):
        for o in LATER[PARTS[e]]:
            part_grads(e, o)
            pair_send(e, o)

    def add_pair(e, parts):
        span = NZ // PARTS[e]
        wait_all(pr.at[e, pl.ds(0, span * len(parts))], "pair", e, parts[0] > 0)
        for o in parts:
            for i in range(span):
                at = span * place(e, o) + i
                pr[e, at] = (pr[e, at].astype(F32) + grads[e, at, c].astype(F32)).astype(BF16)

    def ring_start(e):
        add_pair(e, (0,))
        opposite = mod(z + 4, NZ)
        send(("ru", e, 1), pr.at[e, opposite, pl.ds(0, 32)], ru1.at[e], zdev(1), ("z", e))
        send(("rd", e, 1), pr.at[e, opposite, pl.ds(32, 32)], rd1.at[e], zdev(-1), ("z", e))

    def ring_rest(e):
        add_pair(e, LATER[PARTS[e]])

    def ring(e, k, sign):
        name, one, many = ("ru", ru1, ru) if sign == 1 else ("rd", rd1, rd)
        at = mod(z + sign * (4 - k), NZ)
        wait(name, e, k)
        if k == 1:
            rows = pl.ds(0, 32) if sign == 1 else pl.ds(32, 32)
            pr[e, at, rows] = (pr[e, at, rows].astype(F32) + one[e].astype(F32)).astype(BF16)
        else:
            pr[e, at] = (pr[e, at].astype(F32) + many[k - 2, e].astype(F32)).astype(BF16)
        key = ("end", e) if k == 3 else (name, e, k + 1)
        send(key, pr.at[e, at], many.at[k - 1, e], zdev(sign), ("z", e))

    def put(src, dst, k):
        pltpu.make_async_copy(src, dst, out_sems.at[k]).start()

    def ring_end(e):
        wait_all(pr.at[e, pl.ds(0, 2)], "end", e)
        total = pr[e, z].astype(F32) + ru[2, e].astype(F32) + rd[2, e].astype(F32)
        for i, ref in enumerate((out_gate, out_up, out_down)):
            gout[i, e] = total[:, i * H : (i + 1) * H]
            put(gout.at[i, e], ref.at[e], 1)

    for e in range(NE):
        actions[FWD, e] = lambda e=e: forward(e)
        actions[BWD_A, e] = lambda e=e: backward_first(e)
        actions[BWD_B, e] = lambda e=e: backward_rest(e)
        actions[PAIR_A, e] = lambda e=e: ring_start(e)
        actions[PAIR_B, e] = lambda e=e: ring_rest(e)
        actions[RING_END, e] = lambda e=e: ring_end(e)
        for k in (1, 2, 3):
            actions[RING_UP, e, k] = lambda e=e, k=k: ring(e, k, 1)
            actions[RING_DOWN, e, k] = lambda e=e, k=k: ring(e, k, -1)

    def scatter(n, buf, out, first, lo, group_of_sends):
        dev1, dev2, _ = plane_axes(first)
        blocks = buf.reshape(NY, NX, TOK, D)
        whole = pl.ds(lo, PART)
        halves = (pl.ds(lo, PART // 2), pl.ds(lo + PART // 2, PART // 2))
        local_halves = (pl.ds(0, PART // 2), pl.ds(PART // 2, PART // 2))
        mine, other = (y, x) if first == "y" else (x, y)

        def group(o, at, count):
            if first == "y":
                return blocks.at[mod(mine + o, 4), pl.ds(at, count), whole]
            return blocks.at[pl.ds(at, count), mod(mine + o, 4), whole]

        def own(o, rows):
            if first == "y":
                return blocks.at[mine, mod(other + o, 4), rows]
            return blocks.at[mod(other + o, 4), mine, rows]

        def start():
            yield lambda: send((n, "a1p"), group(2, 0, 2), a1.at[n, 0], dev1(1), group_of_sends)
            yield lambda: send((n, "a1m"), group(2, 2, 2), a1.at[n, 1], dev1(-1), group_of_sends)
            yield lambda: send(
                (n, "a2"), group(1, 2, 2), a2.at[n, 0, pl.ds(2, 2)], dev1(1), group_of_sends
            )
            yield lambda: send(
                (n, "a2"), group(-1, 0, 2), a2.at[n, 1, pl.ds(0, 2)], dev1(-1), group_of_sends
            )

        def add(key, k, o, at, name):
            wait(n, key)
            ref = group(o, at, 2)
            for i in range(2):
                ref[i] = (ref[i].astype(F32) + a1[n, k, i].astype(F32)).astype(BF16)
            send((n, name), ref, a2.at[n, k, pl.ds(at, 2)], dev1(o), group_of_sends)

        def total():
            wait_all(a2.at[n], n, "a2")
            for o in (2, 1, -1, 0):
                ref, at = own(o, whole), mod(other + o, 4)
                ref[...] = (
                    ref[...].astype(F32)
                    + a2[n, 0, at].astype(F32)
                    + a2[n, 1, at].astype(F32)
                ).astype(BF16)
                if o == 2:
                    send((n, "b1p"), own(2, halves[0]), b1.at[n, 0], dev2(1), group_of_sends)
                    send((n, "b1m"), own(2, halves[1]), b1.at[n, 1], dev2(-1), group_of_sends)
                if o == 1:
                    send(
                        (n, "b2"), own(1, halves[1]), b2.at[n, 0, local_halves[1]], dev2(1), group_of_sends
                    )
                if o == -1:
                    send(
                        (n, "b2"), own(-1, halves[0]), b2.at[n, 1, local_halves[0]], dev2(-1), group_of_sends
                    )

        def add_second(key, k, o, name):
            wait(n, key)
            ref = own(o, halves[k])
            ref[...] = (ref[...].astype(F32) + b1[n, k].astype(F32)).astype(BF16)
            send((n, name), ref, b2.at[n, k, local_halves[k]], dev2(o), group_of_sends)

        def finish():
            wait_all(b2.at[n], n, "b2")
            fout[n] = (
                own(0, whole)[...].astype(F32)
                + b2[n, 0].astype(F32)
                + b2[n, 1].astype(F32)
            ).astype(BF16)
            put(fout.at[n], out.at[whole], 0)

        actions[SUM_UP, n] = lambda: add("a1p", 0, 1, 0, "a2")
        actions[SUM_DOWN, n] = lambda: add("a1m", 1, -1, 2, "a2")
        actions[SUM_OWN, n] = total
        actions[LAST_UP, n] = lambda: add_second("b1p", 0, 1, "b2")
        actions[LAST_DOWN, n] = lambda: add_second("b1m", 1, -1, "b2")
        actions[LAST, n] = finish
        return start

    starts = {
        "m": (
            scatter(TA, xbuf, mixed_ref, "y", 0, "m"),
            scatter(TB, xbuf, mixed_ref, "x", PART, "m"),
        ),
        "i": (
            scatter(CA, cbuf, igrad_ref, "x", 0, "i"),
            scatter(CB, cbuf, igrad_ref, "y", PART, "i"),
        ),
    }

    def start_sums(n):
        for one, two in zip(starts[n][0](), starts[n][1]()):
            one()
            two()

    def mix_pair(p, _):
        mixed = dot_nn(weighted_t[p], orow[p])
        xbuf[pl.ds(2 * p, 2)] = mixed.astype(BF16).reshape(2, TOK, D)
        return 0

    def mix_first():
        drain(xbuf.at[pl.ds(0, 15)], "t")
        lax.fori_loop(0, NP // 2, mix_pair, 0, unroll=4)

    def mix():
        lax.fori_loop(NP // 2, NP, mix_pair, 0, unroll=4)
        start_sums("m")

    def gg_copy(i):
        return pltpu.make_async_remote_copy(
            src_ref=gsend.at[lax.rem(ex + i, 16)],
            dst_ref=grecv.at[ex],
            send_sem=gsem_s,
            recv_sem=gsem_r,
            device_id=(dp, lax.rem(ex + i, 16)),
            device_id_type=MESH,
        )

    def gg_start(i, _):
        gg_copy(i).start()
        return 0

    def input_grads():
        drain(cbuf.at[pl.ds(0, 15)], "c")

        def body(p, _):
            back = dot_nn(hot_t[p], rrow[p])
            cbuf[pl.ds(2 * p, 2)] = back.astype(BF16).reshape(2, TOK, D)
            return 0

        lax.fori_loop(0, NP, body, 0, unroll=4)
        start_sums("i")
        lax.fori_loop(1, 16, gg_start, 0)

    actions[(MIX_A,)] = mix_first
    actions[(MIX,)] = mix
    actions[(IGRAD,)] = input_grads

    lax.fori_loop(1, 16, meta_start, 0)
    for name in ORDER:
        actions[name]()

    for sem in (gsem_s, gsem_r):
        pltpu.make_async_copy(grecv.at[pl.ds(0, 15)], grecv.at[pl.ds(0, 15)], sem).wait()
    grecv[ex] = gsend[ex]
    named = routes_ref[...]
    total = jnp.zeros((8, TOK), F32)
    for owner in range(16):
        for j in range(NE):
            total = total + jnp.where(named == NE * owner + j, grecv[owner, j : j + 1, :], 0.0)
    gg_ref[...] = total
    drain(xbuf.at[pl.ds(0, 15)], "m")
    drain(cbuf.at[pl.ds(0, 15)], "i")
    for e in range(NE):
        drain(wbuf.at[e, pl.ds(0, 15)], ("z", e))
    pltpu.make_async_copy(fout, fout, out_sems.at[0]).wait()
    pltpu.make_async_copy(gout, gout, out_sems.at[1]).wait()


def hand_over(*refs):
    held, sems = refs[12:18], refs[18]
    taken = [pltpu.make_async_copy(refs[i], held[i], sems.at[0, i]) for i in range(6)]
    given = [pltpu.make_async_copy(held[i], refs[6 + i], sems.at[1, i]) for i in range(6)]
    for copy in taken:
        copy.start()
    for into, out in zip(taken, given):
        into.wait()
        out.start()
    for copy in given:
        copy.wait()


def step(tokens, cotangent, w_gate, w_up, w_down, routes, gates):
    any_spec = pl.BlockSpec(memory_space=pl.ANY)
    vmem = pl.BlockSpec(memory_space=pltpu.VMEM)
    out = jax.ShapeDtypeStruct
    shapes = (
        out((TOK, D), BF16),
        out((TOK, D), BF16),
        out((8, TOK), F32),
        out((NE, 64, H), F32),
        out((NE, 64, H), F32),
        out((NE, 64, H), F32),
    )
    mixed, igrad, scores, gate, up, down = pl.pallas_call(
        kernel,
        out_shape=shapes,
        in_specs=[any_spec] * 5 + [vmem] * 2,
        out_specs=(any_spec, any_spec, vmem, any_spec, any_spec, any_spec),
        scratch_shapes=[
            pltpu.VMEM((16, TOK, D), BF16),
            pltpu.VMEM((16, TOK, D), BF16),
            pltpu.VMEM((NE, 16, 64, WID), BF16),
            pltpu.VMEM((16, 16, TOK), F32),
            pltpu.VMEM((NE, NP, 2 * TOK), F32),
            pltpu.VMEM((NE, NP, 2 * TOK), F32),
            pltpu.VMEM((NP, NE * PAIR_ROWS, 2 * TOK), BF16),
            pltpu.VMEM((NP, NE * PAIR_ROWS, 2 * TOK), BF16),
            pltpu.VMEM((NP, 2 * TOK, NE * PAIR_ROWS), BF16),
            pltpu.VMEM((NP, 2 * TOK, NE * PAIR_ROWS), BF16),
            pltpu.VMEM((NE, ROWS, D), BF16),
            pltpu.VMEM((NE, ROWS, D), BF16),
            pltpu.VMEM((NE, ROWS, 2 * H), F32),
            pltpu.VMEM((NE, ROWS, H), BF16),
            pltpu.VMEM((NE, ROWS, 2 * H), BF16),
            pltpu.VMEM((NP, NE * PAIR_ROWS, D), BF16),
            pltpu.VMEM((NP, NE * PAIR_ROWS, D), BF16),
            pltpu.VMEM((16, 8, TOK), F32),
            pltpu.VMEM((16, 8, TOK), F32),
            pltpu.VMEM((NE, NZ, 64, WID), BF16),
            pltpu.VMEM((NE, 32, WID), BF16),
            pltpu.VMEM((NE, 32, WID), BF16),
            pltpu.VMEM((3, NE, 64, WID), BF16),
            pltpu.VMEM((3, NE, 64, WID), BF16),
            pltpu.VMEM((4, 2, 2, PART, D), BF16),
            pltpu.VMEM((4, 2, 4, PART, D), BF16),
            pltpu.VMEM((4, 2, PART // 2, D), BF16),
            pltpu.VMEM((4, 2, PART, D), BF16),
            pltpu.VMEM((4, PART, D), BF16),
            pltpu.VMEM((3, NE, 64, H), F32),
            pltpu.SemaphoreType.DMA((12,)),
            pltpu.SemaphoreType.DMA((4 * 12 + 4 * 8 + 4 * 9 + 4 * 6,)),
            pltpu.SemaphoreType.DMA,
            pltpu.SemaphoreType.DMA,
            pltpu.SemaphoreType.DMA,
            pltpu.SemaphoreType.DMA,
            pltpu.SemaphoreType.DMA((3,)),
            pltpu.SemaphoreType.DMA((2,)),
        ],
        compiler_params=pltpu.CompilerParams(
            collective_id=0, has_side_effects=True, vmem_limit_bytes=64 * 1024 * 1024
        ),
    )(tokens, cotangent, w_gate, w_up, w_down, routes, gates)
    mixed, igrad, scores, gate, up, down = pl.pallas_call(
        hand_over,
        out_shape=shapes,
        in_specs=[any_spec] * 6,
        out_specs=(any_spec,) * 6,
        scratch_shapes=[pltpu.VMEM(one.shape, one.dtype) for one in shapes]
        + [pltpu.SemaphoreType.DMA((2, 6))],
    )(mixed, igrad, scores, gate, up, down)
    return mixed, igrad, scores, gate, up, down


def body(tokens, routes, gates, cotangent, w_gate, w_up, w_down):
    mixed, igrad, scores, grad_gate, grad_up, grad_down = step(
        tokens, cotangent, w_gate, w_up, jnp.swapaxes(w_down, 1, 2), routes.T, gates.T
    )
    return (mixed, igrad, scores.T, grad_gate, grad_up, jnp.swapaxes(grad_down, 1, 2))


def solution(mesh):
    rows = P(("dp", "expert"), None)
    features = P("expert", "dp", None)
    last = P("expert", None, "dp")
    return jax.shard_map(
        body,
        mesh=mesh,
        in_specs=(rows, rows, rows, rows, features, features, last),
        out_specs=(rows, rows, rows, features, features, last),
        check_vma=False,
    )
```
